32 devices in a mesh: groups: 2 (over x), member: 2 (over core), tile: 8 (over z, y).
Axes of the slice: x: 2, y: 2, z: 4, core: 2. Of those that a mesh axis runs over, the one named last changes fastest.
Arguments:
- state: float32 [8, 4, 4, 512, 256], P(('groups', 'member'), None, None, 'tile'), parts along dimension 0, may hold values from -6 to 6
- perturbation: float32 [8, 4, 4, 512, 256], P(('groups', 'member'), None, None, 'tile'), parts along dimension 0, may hold values from -2 to 2
- ancestors: int32 [8], P('groups'), parts along dimension 0, may hold values from 0 to 3, as said below
Outputs:
- evolved: float32 [8, 4, 4, 512, 256], P(('groups', 'member'), None, None, 'tile'), parts along dimension 0
- observable: float32 [8], P(('groups', 'member')), parts along dimension 0
The draws below stay inside these ranges and needn't reach their ends.
There are 2 independent parts, one for each index of `groups`. The reference program is written for one: setup_inputs(seed, part) draws one part's arguments, and reference() takes and returns one part's arrays. A program takes and returns all parts, laid end to end along the dimension named above; each array names one. Nothing has to cross between parts.
Inputs may be any that keep to these rules, and one draw needn't show every extreme that they name: `ancestors`: surviving slots name themselves; every other slot names a surviving slot; at least two slots survive and at least one does not.
All inputs are finite; a program needn't handle non-finite values.
Results may differ from the reference program's by a relative error of at most 0.00002.
Values sent between devices are 32-bit elements; how exact they have to be, the bound alone decides.
A program may use at most 64 MiB of HBM per device.

```python
import jax
import jax.numpy as jnp

COLUMNS = 256
LEVELS = 4
FIELDS = 4
STEPS_EACH = 2
ENSEMBLE_SIZE = 4
ROWS = 512


def draw_ancestors(key, part):
    key_order = jax.random.fold_in(key, 11)
    count_key = jax.random.fold_in(key, 12)
    picking_key = jax.random.fold_in(key, 13)
    order = jax.random.permutation(key_order, ENSEMBLE_SIZE).astype(jnp.int32)
    member_ranks = jnp.argsort(order, stable=True).astype(jnp.int32)
    kept_members = jax.random.randint(count_key, (), 2, ENSEMBLE_SIZE, dtype=jnp.int32)
    living_members = member_ranks < kept_members
    chosen_members = jax.random.randint(picking_key, (ENSEMBLE_SIZE,), 0, kept_members, dtype=jnp.int32)
    sources = jnp.take(order, chosen_members)
    return jnp.where(living_members, jnp.arange(ENSEMBLE_SIZE, dtype=jnp.int32), sources).astype(jnp.int32)


def block_scale(rng, extent, cuts, least, high):
    gain, own = 1.0, jax.random.fold_in(rng, 6)
    for dim, shards_of in cuts:
        steps = jnp.exp(jax.random.uniform(jax.random.fold_in(own, dim), (shards_of,), jnp.float32, least / len(cuts), high / len(cuts)))
        gain = gain * jnp.repeat(steps, extent[dim] // shards_of).reshape([-1 if axis == dim else 1 for axis in range(len(extent))])
    return gain


def normal_values(key, extent, scale, reach, split=(), held_as=jnp.bfloat16):
    array = scale * jax.random.normal(key, extent, jnp.float32)
    if split:
        array = array * block_scale(key, extent, split, -0.22, 0.18)
    return jnp.clip(array, -reach, reach).astype(held_as)


def setup_inputs(seed: int = 0, part: int = 0) -> dict:
    arg_keys = jax.random.split(jax.random.key(seed), 4)
    part_keys = jax.random.split(jax.random.fold_in(arg_keys[3], part), 4)
    state = normal_values(part_keys[0], (ENSEMBLE_SIZE, FIELDS, LEVELS, ROWS, COLUMNS), 1.0, 6.0, ((0, 2), (3, 8)), jnp.float32)
    perturbation = normal_values(part_keys[1], (ENSEMBLE_SIZE, FIELDS, LEVELS, ROWS, COLUMNS), 0.3, 2.0, ((0, 2), (3, 8)), jnp.float32)
    ancestors = draw_ancestors(jax.random.fold_in(jax.random.fold_in(arg_keys[3], part), 71), part)
    return {"state": state, "perturbation": perturbation, "ancestors": ancestors}


TIME_STEP = 0.15
DIFFUSION = 0.2
MIXING = 0.1
CORIOLIS = 0.5
BUOYANCY_GAIN = 0.3
STRATIFICATION = 0.3
SATURATION = 0.5
LATENT = 0.5


def advance_core(padded):
    centre = padded[:, :, :, 2:-2, :]
    north_one = padded[:, :, :, 3:-1, :]
    south_one = padded[:, :, :, 1:-3, :]
    north_two = padded[:, :, :, 4:, :]
    south_two = padded[:, :, :, :-4, :]
    east_one = jnp.roll(centre, -1, axis=4)
    west_one = jnp.roll(centre, 1, axis=4)
    east_two = jnp.roll(centre, -2, axis=4)
    west_two = jnp.roll(centre, 2, axis=4)
    slope_y = (8.0 * (north_one - south_one) - (north_two - south_two)) / 12.0
    slope_x = (8.0 * (east_one - west_one) - (east_two - west_two)) / 12.0
    laplace = north_one + south_one + east_one + west_one - 4.0 * centre
    upper = jnp.concatenate([centre[:, :, 1:], centre[:, :, -1:]], axis=2)
    lower = jnp.concatenate([centre[:, :, :1], centre[:, :, :-1]], axis=2)
    vertical = upper + lower - 2.0 * centre
    east_wind = centre[:, 0:1]
    north_wind = centre[:, 1:2]
    buoyancy = centre[:, 2:3]
    tendency = -(east_wind * slope_x + north_wind * slope_y) + DIFFUSION * laplace + MIXING * vertical
    forcing = jnp.concatenate([CORIOLIS * north_wind, -CORIOLIS * east_wind + BUOYANCY_GAIN * buoyancy,
                               -STRATIFICATION * north_wind, jnp.zeros_like(north_wind)], axis=1)
    updated = centre + TIME_STEP * (tendency + forcing)
    buoyancy_new = updated[:, 2:3]
    moisture = updated[:, 3:4]
    excess = jnp.maximum(moisture - SATURATION * jnp.exp(0.1 * buoyancy_new), 0.0)
    return jnp.concatenate([updated[:, 0:2], buoyancy_new + LATENT * excess, moisture - excess], axis=1)


def advance_all(fields):
    for number in range(STEPS_EACH):
        fields = advance_core(jnp.pad(fields, ((0, 0), (0, 0), (0, 0), (2, 2), (0, 0))))
    return fields


def reference(state, perturbation, ancestors):
    fields = advance_all(state)
    fields = jnp.take(fields, ancestors.astype(jnp.int32), axis=0) + perturbation
    fields = advance_all(fields)
    rows_all = fields.shape[3]
    latitude = jnp.arange(rows_all).astype(jnp.float32)
    weight = 1.0 + 2.0 * latitude / (rows_all - 1)
    buoyancy = fields[:, 2]
    total = jnp.sum(weight[:, None] * buoyancy * buoyancy, axis=(1, 2, 3))
    observable = total / (fields.shape[2] * rows_all * fields.shape[4])
    return fields, observable
```

```python
import functools

import jax
import jax.numpy as jnp
from jax import lax
from jax.experimental import pallas as pl
from jax.experimental.pallas import tpu as pltpu
from jax.sharding import PartitionSpec as P

TIME_STEP = 0.15
DIFFUSION = 0.2
MIXING = 0.1
CORIOLIS = 0.5
BUOYANCY_GAIN = 0.3
STRATIFICATION = 0.3
SATURATION = 0.5
LATENT = 0.5

LANES = 128
PAD = 8
MESH = pl.DeviceIdType.MESH


def advance_block(load, emit, halves, levels):
    spread = TIME_STEP * DIFFUSION
    mix = TIME_STEP * MIXING
    keep = 1.0 - TIME_STEP * (4.0 * DIFFUSION + 2.0 * MIXING)
    lane = lax.broadcasted_iota(jnp.int32, (8, LANES), 1)

    def shifted(parts, k):
        turned = [pltpu.roll(part, k % LANES, 1) for part in parts]
        wrapped = (lane >= LANES + k) if k < 0 else (lane < k)
        step = 1 if k < 0 else -1
        return [jnp.where(wrapped, turned[(h + step) % halves], turned[h]) for h in range(halves)]

    for level in range(levels):
        centre = [[load(field, level, h, 0) for h in range(halves)] for field in range(4)]
        weights = []
        for h in range(halves):
            east, north = centre[0][h], centre[1][h]
            east_eight = east * (TIME_STEP * 8.0 / 12.0)
            north_eight = north * (TIME_STEP * 8.0 / 12.0)
            weights.append((
                east * (TIME_STEP / 12.0), spread - east_eight, spread + east_eight,
                north * (TIME_STEP / 12.0), spread - north_eight, spread + north_eight,
            ))
        updated = []
        for field in range(4):
            e1, w1, e2, w2 = [shifted(centre[field], k) for k in (-1, 1, -2, 2)]
            news = []
            for h in range(halves):
                east_far, east_near, west_near, north_far, north_near, south_near = weights[h]
                c = centre[field][h]
                n1, s1, n2, s2 = [load(field, level, h, k) for k in (1, -1, 2, -2)]
                edge = (level == 0) + (level == levels - 1)
                beside = [load(field, other, h, 0) for other in (level - 1, level + 1) if 0 <= other < levels]
                new = c * (keep + edge * mix)
                if beside:
                    new = new + functools.reduce(jnp.add, beside) * mix
                new = new + ((e1[h] * east_near + w1[h] * west_near) + (e2[h] - w2[h]) * east_far)
                new = new + ((n1 * north_near + s1 * south_near) + (n2 - s2) * north_far)
                if field == 0:
                    new = new + (TIME_STEP * CORIOLIS) * centre[1][h]
                elif field == 1:
                    new = new + ((TIME_STEP * BUOYANCY_GAIN) * centre[2][h] - (TIME_STEP * CORIOLIS) * centre[0][h])
                elif field == 2:
                    new = new - (TIME_STEP * STRATIFICATION) * centre[1][h]
                news.append(new)
            updated.append(news)
        for h in range(halves):
            excess = jnp.maximum(updated[3][h] - SATURATION * jnp.exp(0.1 * updated[2][h]), 0.0)
            emit(0, level, h, updated[0][h])
            emit(1, level, h, updated[1][h])
            emit(2, level, h, updated[2][h] + LATENT * excess)
            emit(3, level, h, updated[3][h] - excess)


def kernel(tiles, ancestors, state, pert, out, means,
           a, b, early_mid, early_edge, r, p, send1, recv1, send2, recv2, mine, landed,
           load_sem, pert_sem, edge_send, edge_recv, mid_send, mid_recv,
           clone_send, clone_recv, sum_send, sum_recv):
    slots, fields, levels, rows, columns = state.shape
    halves = columns // LANES
    t = lax.axis_index("tile")
    m = lax.axis_index("member")
    has_lo = t > 0
    has_hi = t < tiles - 1
    partner = {"member": 1 - m}
    below = {"tile": t - 1}
    above = {"tile": t + 1}
    inner = rows - 16
    last = rows - 8

    parts = ((0, 8), (last, 8), (8, inner))

    def load_copy(s, part, h):
        start, size = parts[part]
        return pltpu.make_async_copy(
            state.at[s, :, :, pl.ds(start, size), pl.ds(h * LANES, LANES)],
            a.at[s, :, :, h, pl.ds(PAD + start, size), :], load_sem.at[s, part, h])

    def pert_copy(s, h):
        return pltpu.make_async_copy(
            pert.at[s, :, :, :, pl.ds(h * LANES, LANES)], p.at[s, :, :, h], pert_sem.at[s, h])

    for part in range(3):
        for s in range(slots):
            for h in range(halves):
                load_copy(s, part, h).start()
    for s in range(slots):
        for h in range(halves):
            pert_copy(s, h).start()

    barrier = pltpu.get_barrier_semaphore()
    pl.semaphore_signal(barrier, inc=1, device_id=partner, device_id_type=MESH)
    for step in range(1, tiles):
        peer = {"tile": lax.rem(t + step, tiles)}
        pl.semaphore_signal(barrier, inc=1, device_id=peer, device_id_type=MESH)

    def remote(src, dst, ssem, rsem, where):
        return pltpu.make_async_remote_copy(
            src_ref=src, dst_ref=dst, send_sem=ssem, recv_sem=rsem, device_id=where, device_id_type=MESH)

    sub = lax.broadcasted_iota(jnp.int32, (8, LANES), 0)

    def pack(src, dst, s):
        for side, at in ((0, PAD), (1, PAD + rows - 4)):
            for field in range(fields):
                for pair in range(levels // 2):
                    for h in range(halves):
                        low = src[s, field, 2 * pair, h, pl.ds(at, 8), :]
                        high = src[s, field, 2 * pair + 1, h, pl.ds(at - 4, 8), :]
                        dst[s, side, field, pair, h] = jnp.where(sub < 4, low, high)

    def unpack(src, dst, s):
        for side, has, at in ((0, has_hi, PAD + rows), (1, has_lo, 0)):
            @pl.when(has)
            def _():
                for field in range(fields):
                    for pair in range(levels // 2):
                        for h in range(halves):
                            tile = src[s, side, field, pair, h]
                            turned = pltpu.roll(tile, 4, 0)
                            first, second = (tile, turned) if side == 0 else (turned, tile)
                            dst[s, field, 2 * pair, h, pl.ds(at, 8), :] = first
                            dst[s, field, 2 * pair + 1, h, pl.ds(at, 8), :] = second

            @pl.when(jnp.logical_not(has))
            def _():
                dst[s, :, :, :, pl.ds(at, 8), :] = jnp.zeros((fields, levels, halves, 8, LANES), jnp.float32)

    def edge_copies(number, src, dst, s):
        return [
            (remote(src.at[s, 0], dst.at[s, 0], edge_send.at[number, s, 0], edge_recv.at[number, s, 0], below), has_lo, has_hi),
            (remote(src.at[s, 1], dst.at[s, 1], edge_send.at[number, s, 1], edge_recv.at[number, s, 1], above), has_hi, has_lo),
        ]

    def start_edges(*args):
        for copy, sends, _ in edge_copies(*args):
            pl.when(sends)(copy.start)

    def wait_edges(*args):
        for copy, _, receives in edge_copies(*args):
            pl.when(receives)(copy.wait_recv)

    def finish_edges(*args):
        for copy, sends, _ in edge_copies(*args):
            pl.when(sends)(copy.wait_send)

    def blocks(count, first, stride, src, s, emit_at):
        def one(i, none):
            row = first + i * stride

            def load(field, level, h, shift):
                return src[s, field, level, h, pl.ds(PAD + row + shift, 8), :]

            advance_block(load, functools.partial(emit_at, i, row), halves, levels)
            return none

        lax.fori_loop(0, count, one, 0)

    def into_b(s):
        def emit_at(i, row, field, level, h, value):
            b[s, field, level, h, pl.ds(PAD + row, 8), :] = value
        return emit_at

    def clear_b(s):
        zero = jnp.zeros((fields, levels, halves, 8, LANES), jnp.float32)

        @pl.when(jnp.logical_not(has_lo))
        def _():
            b[s, :, :, :, pl.ds(0, 8), :] = zero

        @pl.when(jnp.logical_not(has_hi))
        def _():
            b[s, :, :, :, pl.ds(PAD + rows, 8), :] = zero

    for s in range(slots):
        for part in range(2):
            for h in range(halves):
                load_copy(s, part, h).wait()
    lax.fori_loop(0, slots, lambda s, c: (pack(a, send1, s), c)[1], 0)
    pl.semaphore_wait(barrier, tiles)
    for s in range(slots):
        start_edges(0, send1, recv1, s)

    def mid_copy(s):
        own = m * slots + s
        return remote(early_mid.at[own], early_mid.at[own], mid_send.at[s], mid_recv.at[s], partner)

    def early_inner(s, carry):
        for h in range(halves):
            load_copy(s, 2, h).wait()
        blocks((rows - 8) // 8, 2, 8, a, s, into_b(s))

        def emit_at(i, row, field, level, h, value):
            early_mid[m * slots + s, field, level, h, pl.ds(pl.multiple_of(i * 8, 8), 8), :] = value

        blocks(inner // 8, 8, 8, b, s, emit_at)
        mid_copy(s).start()
        return carry

    lax.fori_loop(0, slots, early_inner, 0)

    def clone_copy(s):
        own = m * slots + s
        return remote(early_edge.at[own], early_edge.at[own], clone_send.at[s], clone_recv.at[s], partner)

    def early_outer(s, carry):
        wait_edges(0, send1, recv1, s)
        unpack(recv1, a, s)
        blocks(2, -2, rows - 4, a, s, into_b(s))
        clear_b(s)

        def emit_at(i, row, field, level, h, value):
            early_edge[m * slots + s, i, field, level, h] = value

        blocks(2, 0, last, b, s, emit_at)
        clone_copy(s).start()
        return carry

    lax.fori_loop(0, slots, early_outer, 0)

    for s in range(slots):
        for h in range(halves):
            pert_copy(s, h).wait()
    for s in range(slots):
        clone_copy(s).wait_recv()

    def restart_outer(s, carry):
        source = ancestors[m * slots + s]
        for i, at in ((0, 0), (1, last)):
            for field in range(fields):
                for level in range(levels):
                    for h in range(halves):
                        r[s, field, level, h, pl.ds(PAD + at, 8), :] = (
                            early_edge[source, i, field, level, h] + p[s, field, level, h, pl.ds(at, 8), :])
        pack(r, send2, s)
        start_edges(1, send2, recv2, s)
        return carry

    lax.fori_loop(0, slots, restart_outer, 0)
    for s in range(slots):
        mid_copy(s).wait_recv()

    sums = [[jnp.zeros((8, LANES), jnp.float32)] for _ in range(slots)]

    def into_out(s):
        def emit_at(i, row, field, level, h, value):
            out[s, field, level, pl.ds(pl.multiple_of(row, 8), 8), pl.ds(h * LANES, LANES)] = value
            if field == 2:
                place = lax.broadcasted_iota(jnp.int32, (8, LANES), 0) + (t * rows + row)
                weight = 1.0 + 2.0 * place.astype(jnp.float32) / (tiles * rows - 1)
                mine[s] = mine[s] + weight * (value * value)
        return emit_at

    def late_inner(s, carry):
        source = ancestors[m * slots + s]

        def add(i, none):
            row = pl.multiple_of(i * 8, 8)
            for field in range(fields):
                for level in range(levels):
                    for h in range(halves):
                        r[s, field, level, h, pl.ds(PAD + 8 + row, 8), :] = (
                            early_mid[source, field, level, h, pl.ds(row, 8), :]
                            + p[s, field, level, h, pl.ds(8 + row, 8), :])
            return none

        lax.fori_loop(0, inner // 8, add, 0)
        mine[s] = jnp.zeros((8, LANES), jnp.float32)
        blocks((rows - 8) // 8, 2, 8, r, s, into_b(s))
        blocks(inner // 8, 8, 8, b, s, into_out(s))
        return carry

    lax.fori_loop(0, slots, late_inner, 0)

    def late_outer(s, carry):
        wait_edges(1, send2, recv2, s)
        unpack(recv2, r, s)
        blocks(2, -2, rows - 4, r, s, into_b(s))
        clear_b(s)
        blocks(2, 0, last, b, s, into_out(s))
        return carry

    lax.fori_loop(0, slots, late_outer, 0)

    sends = [
        remote(mine, landed.at[step - 1], sum_send.at[step - 1], sum_recv.at[step - 1], {"tile": lax.rem(t + step, tiles)})
        for step in range(1, tiles)
    ]
    for copy in sends:
        copy.start()
    for s in range(slots):
        for number, src, dst in ((0, send1, recv1), (1, send2, recv2)):
            finish_edges(number, src, dst, s)
        mid_copy(s).wait_send()
        clone_copy(s).wait_send()
    for copy in sends:
        copy.wait()
    scale = 1.0 / (levels * tiles * rows * columns)
    for s in range(slots):
        total = mine[s]
        for step in range(tiles - 1):
            total = total + landed[step, s]
        means[s] = jnp.sum(total) * scale


def body(state, pert, ancestors):
    slots, fields, levels, rows, columns = state.shape
    tiles = lax.axis_size("tile")
    halves = columns // LANES
    members = ancestors.shape[0]
    tall = (slots, fields, levels, halves, rows + 2 * PAD, LANES)
    edge = (slots, 2, fields, levels // 2, halves, 8, LANES)
    f32 = lambda *shape: pltpu.VMEM(shape, jnp.float32)
    dma = lambda *shape: pltpu.SemaphoreType.DMA(shape)
    anywhere = pl.BlockSpec(memory_space=pl.ANY)
    return pl.pallas_call(
        functools.partial(kernel, tiles),
        out_shape=[
            jax.ShapeDtypeStruct(state.shape, jnp.float32),
            jax.ShapeDtypeStruct((slots,), jnp.float32),
        ],
        in_specs=[pl.BlockSpec(memory_space=pltpu.SMEM), anywhere, anywhere],
        out_specs=[pl.BlockSpec(memory_space=pltpu.VMEM), pl.BlockSpec(memory_space=pltpu.SMEM)],
        scratch_shapes=[
            f32(*tall), f32(*tall),
            f32(members, fields, levels, halves, rows - 16, LANES),
            f32(members, 2, fields, levels, halves, 8, LANES),
            f32(*tall),
            f32(slots, fields, levels, halves, rows, LANES),
            f32(*edge), f32(*edge), f32(*edge), f32(*edge),
            f32(slots, 8, LANES), f32(tiles - 1, slots, 8, LANES),
            dma(slots, 3, halves), dma(slots, halves),
            dma(2, slots, 2), dma(2, slots, 2),
            dma(slots), dma(slots), dma(slots), dma(slots),
            dma(tiles - 1), dma(tiles - 1),
        ],
        compiler_params=pltpu.CompilerParams(
            collective_id=0, has_side_effects=True, vmem_limit_bytes=48 << 20),
        name="event",
    )(ancestors, state, pert)


def solution(mesh):
    spec = P(("groups", "member"), None, None, "tile", None)
    return jax.shard_map(
        body,
        mesh=mesh,
        in_specs=(spec, spec, P("groups")),
        out_specs=(spec, P(("groups", "member"))),
        check_vma=False,
    )
```

```python
import functools

import jax
import jax.numpy as jnp
from jax import lax
from jax.experimental import pallas as pl
from jax.experimental.pallas import tpu as pltpu
from jax.sharding import PartitionSpec as P

TIME_STEP = 0.15
DIFFUSION = 0.2
MIXING = 0.1
CORIOLIS = 0.5
BUOYANCY_GAIN = 0.3
STRATIFICATION = 0.3
SATURATION = 0.5
LATENT = 0.5

LANES = 128
PAD = 8
MESH = pl.DeviceIdType.MESH


def advance_block(load, emit, halves, levels):
    spread = TIME_STEP * DIFFUSION
    mix = TIME_STEP * MIXING
    keep = 1.0 - TIME_STEP * (4.0 * DIFFUSION + 2.0 * MIXING)
    lane = lax.broadcasted_iota(jnp.int32, (8, LANES), 1)

    def shifted(parts, k):
        turned = [pltpu.roll(part, k % LANES, 1) for part in parts]
        wrapped = (lane >= LANES + k) if k < 0 else (lane < k)
        step = 1 if k < 0 else -1
        return [jnp.where(wrapped, turned[(h + step) % halves], turned[h]) for h in range(halves)]

    for level in range(levels):
        centre = [[load(field, level, h, 0) for h in range(halves)] for field in range(4)]
        weights = []
        for h in range(halves):
            east, north = centre[0][h], centre[1][h]
            east_eight = east * (TIME_STEP * 8.0 / 12.0)
            north_eight = north * (TIME_STEP * 8.0 / 12.0)
            weights.append((
                east * (TIME_STEP / 12.0), spread - east_eight, spread + east_eight,
                north * (TIME_STEP / 12.0), spread - north_eight, spread + north_eight,
            ))
        updated = []
        for field in range(4):
            e1, w1, e2, w2 = [shifted(centre[field], k) for k in (-1, 1, -2, 2)]
            news = []
            for h in range(halves):
                east_far, east_near, west_near, north_far, north_near, south_near = weights[h]
                c = centre[field][h]
                n1, s1, n2, s2 = [load(field, level, h, k) for k in (1, -1, 2, -2)]
                edge = (level == 0) + (level == levels - 1)
                beside = [load(field, other, h, 0) for other in (level - 1, level + 1) if 0 <= other < levels]
                new = c * (keep + edge * mix)
                if beside:
                    new = new + functools.reduce(jnp.add, beside) * mix
                new = new + ((e1[h] * east_near + w1[h] * west_near) + (e2[h] - w2[h]) * east_far)
                new = new + ((n1 * north_near + s1 * south_near) + (n2 - s2) * north_far)
                if field == 0:
                    new = new + (TIME_STEP * CORIOLIS) * centre[1][h]
                elif field == 1:
                    new = new + ((TIME_STEP * BUOYANCY_GAIN) * centre[2][h] - (TIME_STEP * CORIOLIS) * centre[0][h])
                elif field == 2:
                    new = new - (TIME_STEP * STRATIFICATION) * centre[1][h]
                news.append(new)
            updated.append(news)
        for h in range(halves):
            excess = jnp.maximum(updated[3][h] - SATURATION * jnp.exp(0.1 * updated[2][h]), 0.0)
            emit(0, level, h, updated[0][h])
            emit(1, level, h, updated[1][h])
            emit(2, level, h, updated[2][h] + LATENT * excess)
            emit(3, level, h, updated[3][h] - excess)


def kernel(tiles, names, state, pert, out, means,
           ancestors, a, b, early_mid, early_edge, r, p, send1, recv1, send2, recv2, mine, landed,
           name_sem, load_sem, pert_sem, edge_send, edge_recv, mid_send, mid_recv,
           clone_send, clone_recv, sum_send, sum_recv):
    slots, fields, levels, rows, columns = state.shape
    halves = columns // LANES
    t = lax.axis_index("tile")
    m = lax.axis_index("member")
    has_lo = t > 0
    has_hi = t < tiles - 1
    partner = {"member": 1 - m}
    below = {"tile": t - 1}
    above = {"tile": t + 1}
    inner = rows - 16
    last = rows - 8

    parts = ((0, 8), (last, 8), (8, inner))

    def load_copy(s, part, h):
        start, size = parts[part]
        return pltpu.make_async_copy(
            state.at[s, :, :, pl.ds(start, size), pl.ds(h * LANES, LANES)],
            a.at[s, :, :, h, pl.ds(PAD + start, size), :], load_sem.at[s, part, h])

    def pert_copy(s, h):
        return pltpu.make_async_copy(
            pert.at[s, :, :, :, pl.ds(h * LANES, LANES)], p.at[s, :, :, h], pert_sem.at[s, h])

    for part in range(3):
        for s in range(slots):
            for h in range(halves):
                load_copy(s, part, h).start()
    for s in range(slots):
        for h in range(halves):
            pert_copy(s, h).start()
    name_copy = pltpu.make_async_copy(names, ancestors, name_sem)
    name_copy.start()

    barrier = pltpu.get_barrier_semaphore()
    pl.semaphore_signal(barrier, inc=1, device_id=partner, device_id_type=MESH)
    for step in range(1, tiles):
        peer = {"tile": lax.rem(t + step, tiles)}
        pl.semaphore_signal(barrier, inc=1, device_id=peer, device_id_type=MESH)

    def remote(src, dst, ssem, rsem, where):
        return pltpu.make_async_remote_copy(
            src_ref=src, dst_ref=dst, send_sem=ssem, recv_sem=rsem, device_id=where, device_id_type=MESH)

    sub = lax.broadcasted_iota(jnp.int32, (8, LANES), 0)

    def pack(src, dst, s):
        for side, at in ((0, PAD), (1, PAD + rows - 4)):
            for field in range(fields):
                for pair in range(levels // 2):
                    for h in range(halves):
                        low = src[s, field, 2 * pair, h, pl.ds(at, 8), :]
                        high = src[s, field, 2 * pair + 1, h, pl.ds(at - 4, 8), :]
                        dst[s, side, field, pair, h] = jnp.where(sub < 4, low, high)

    def unpack(src, dst, s):
        for side, has, at in ((0, has_hi, PAD + rows), (1, has_lo, 0)):
            @pl.when(has)
            def _():
                for field in range(fields):
                    for pair in range(levels // 2):
                        for h in range(halves):
                            tile = src[s, side, field, pair, h]
                            turned = pltpu.roll(tile, 4, 0)
                            first, second = (tile, turned) if side == 0 else (turned, tile)
                            dst[s, field, 2 * pair, h, pl.ds(at, 8), :] = first
                            dst[s, field, 2 * pair + 1, h, pl.ds(at, 8), :] = second

            @pl.when(jnp.logical_not(has))
            def _():
                dst[s, :, :, :, pl.ds(at, 8), :] = jnp.zeros((fields, levels, halves, 8, LANES), jnp.float32)

    def edge_copies(number, src, dst, s):
        return [
            (remote(src.at[s, 0], dst.at[s, 0], edge_send.at[number, s, 0], edge_recv.at[number, s, 0], below), has_lo, has_hi),
            (remote(src.at[s, 1], dst.at[s, 1], edge_send.at[number, s, 1], edge_recv.at[number, s, 1], above), has_hi, has_lo),
        ]

    def start_edges(*args):
        for copy, sends, _ in edge_copies(*args):
            pl.when(sends)(copy.start)

    def wait_edges(*args):
        for copy, _, receives in edge_copies(*args):
            pl.when(receives)(copy.wait_recv)

    def finish_edges(*args):
        for copy, sends, _ in edge_copies(*args):
            pl.when(sends)(copy.wait_send)

    def blocks(count, first, stride, src, s, emit_at):
        def one(i, none):
            row = first + i * stride

            def load(field, level, h, shift):
                return src[s, field, level, h, pl.ds(PAD + row + shift, 8), :]

            advance_block(load, functools.partial(emit_at, i, row), halves, levels)
            return none

        lax.fori_loop(0, count, one, 0)

    def into_b(s):
        def emit_at(i, row, field, level, h, value):
            b[s, field, level, h, pl.ds(PAD + row, 8), :] = value
        return emit_at

    def clear_b(s):
        zero = jnp.zeros((fields, levels, halves, 8, LANES), jnp.float32)

        @pl.when(jnp.logical_not(has_lo))
        def _():
            b[s, :, :, :, pl.ds(0, 8), :] = zero

        @pl.when(jnp.logical_not(has_hi))
        def _():
            b[s, :, :, :, pl.ds(PAD + rows, 8), :] = zero

    for s in range(slots):
        for part in range(2):
            for h in range(halves):
                load_copy(s, part, h).wait()
    lax.fori_loop(0, slots, lambda s, c: (pack(a, send1, s), c)[1], 0)
    pl.semaphore_wait(barrier, tiles)
    for s in range(slots):
        start_edges(0, send1, recv1, s)

    def mid_copy(s):
        own = m * slots + s
        return remote(early_mid.at[own], early_mid.at[own], mid_send.at[s], mid_recv.at[s], partner)

    def early_inner(s, carry):
        for h in range(halves):
            load_copy(s, 2, h).wait()
        blocks((rows - 8) // 8, 2, 8, a, s, into_b(s))

        def emit_at(i, row, field, level, h, value):
            early_mid[m * slots + s, field, level, h, pl.ds(pl.multiple_of(i * 8, 8), 8), :] = value

        blocks(inner // 8, 8, 8, b, s, emit_at)
        mid_copy(s).start()
        return carry

    lax.fori_loop(0, slots, early_inner, 0)

    def clone_copy(s):
        own = m * slots + s
        return remote(early_edge.at[own], early_edge.at[own], clone_send.at[s], clone_recv.at[s], partner)

    def early_outer(s, carry):
        wait_edges(0, send1, recv1, s)
        unpack(recv1, a, s)
        blocks(2, -2, rows - 4, a, s, into_b(s))
        clear_b(s)

        def emit_at(i, row, field, level, h, value):
            early_edge[m * slots + s, i, field, level, h] = value

        blocks(2, 0, last, b, s, emit_at)
        clone_copy(s).start()
        return carry

    lax.fori_loop(0, slots, early_outer, 0)

    name_copy.wait()
    for s in range(slots):
        for h in range(halves):
            pert_copy(s, h).wait()
    for s in range(slots):
        clone_copy(s).wait_recv()

    def restart_outer(s, carry):
        source = ancestors[m * slots + s]
        for i, at in ((0, 0), (1, last)):
            for field in range(fields):
                for level in range(levels):
                    for h in range(halves):
                        r[s, field, level, h, pl.ds(PAD + at, 8), :] = (
                            early_edge[source, i, field, level, h] + p[s, field, level, h, pl.ds(at, 8), :])
        pack(r, send2, s)
        start_edges(1, send2, recv2, s)
        return carry

    lax.fori_loop(0, slots, restart_outer, 0)
    for s in range(slots):
        mid_copy(s).wait_recv()

    sums = [[jnp.zeros((8, LANES), jnp.float32)] for _ in range(slots)]

    def into_out(s):
        def emit_at(i, row, field, level, h, value):
            out[s, field, level, pl.ds(pl.multiple_of(row, 8), 8), pl.ds(h * LANES, LANES)] = value
            if field == 2:
                place = lax.broadcasted_iota(jnp.int32, (8, LANES), 0) + (t * rows + row)
                weight = 1.0 + 2.0 * place.astype(jnp.float32) / (tiles * rows - 1)
                mine[s] = mine[s] + weight * (value * value)
        return emit_at

    def late_inner(s, carry):
        source = ancestors[m * slots + s]

        def add(i, none):
            row = pl.multiple_of(i * 8, 8)
            for field in range(fields):
                for level in range(levels):
                    for h in range(halves):
                        r[s, field, level, h, pl.ds(PAD + 8 + row, 8), :] = (
                            early_mid[source, field, level, h, pl.ds(row, 8), :]
                            + p[s, field, level, h, pl.ds(8 + row, 8), :])
            return none

        lax.fori_loop(0, inner // 8, add, 0)
        mine[s] = jnp.zeros((8, LANES), jnp.float32)
        blocks((rows - 8) // 8, 2, 8, r, s, into_b(s))
        blocks(inner // 8, 8, 8, b, s, into_out(s))
        return carry

    lax.fori_loop(0, slots, late_inner, 0)

    def late_outer(s, carry):
        wait_edges(1, send2, recv2, s)
        unpack(recv2, r, s)
        blocks(2, -2, rows - 4, r, s, into_b(s))
        clear_b(s)
        blocks(2, 0, last, b, s, into_out(s))
        return carry

    lax.fori_loop(0, slots, late_outer, 0)

    sends = [
        remote(mine, landed.at[step - 1], sum_send.at[step - 1], sum_recv.at[step - 1], {"tile": lax.rem(t + step, tiles)})
        for step in range(1, tiles)
    ]
    for copy in sends:
        copy.start()
    for s in range(slots):
        for number, src, dst in ((0, send1, recv1), (1, send2, recv2)):
            finish_edges(number, src, dst, s)
        mid_copy(s).wait_send()
        clone_copy(s).wait_send()
    for copy in sends:
        copy.wait()
    scale = 1.0 / (levels * tiles * rows * columns)
    for s in range(slots):
        total = mine[s]
        for step in range(tiles - 1):
            total = total + landed[step, s]
        means[s] = jnp.sum(total) * scale


def body(state, pert, ancestors):
    slots, fields, levels, rows, columns = state.shape
    tiles = lax.axis_size("tile")
    halves = columns // LANES
    members = ancestors.shape[0]
    tall = (slots, fields, levels, halves, rows + 2 * PAD, LANES)
    edge = (slots, 2, fields, levels // 2, halves, 8, LANES)
    f32 = lambda *shape: pltpu.VMEM(shape, jnp.float32)
    dma = lambda *shape: pltpu.SemaphoreType.DMA(shape)
    outside = pl.BlockSpec(memory_space=pltpu.HBM)
    return pl.pallas_call(
        functools.partial(kernel, tiles),
        out_shape=[
            jax.ShapeDtypeStruct(state.shape, jnp.float32),
            jax.ShapeDtypeStruct((slots,), jnp.float32),
        ],
        in_specs=[outside] * 3,
        out_specs=[pl.BlockSpec(memory_space=pltpu.VMEM), pl.BlockSpec(memory_space=pltpu.SMEM)],
        scratch_shapes=[
            pltpu.SMEM((members,), jnp.int32),
            f32(*tall), f32(*tall),
            f32(members, fields, levels, halves, rows - 16, LANES),
            f32(members, 2, fields, levels, halves, 8, LANES),
            f32(*tall),
            f32(slots, fields, levels, halves, rows, LANES),
            f32(*edge), f32(*edge), f32(*edge), f32(*edge),
            f32(slots, 8, LANES), f32(tiles - 1, slots, 8, LANES),
            pltpu.SemaphoreType.DMA, dma(slots, 3, halves), dma(slots, halves),
            dma(2, slots, 2), dma(2, slots, 2),
            dma(slots), dma(slots), dma(slots), dma(slots),
            dma(tiles - 1), dma(tiles - 1),
        ],
        compiler_params=pltpu.CompilerParams(
            collective_id=0, has_side_effects=True, vmem_limit_bytes=48 << 20),
        name="event",
    )(*[pltpu.with_memory_space_constraint(x, pltpu.HBM) for x in (ancestors, state, pert)])


def solution(mesh):
    spec = P(("groups", "member"), None, None, "tile", None)
    return jax.shard_map(
        body,
        mesh=mesh,
        in_specs=(spec, spec, P("groups")),
        out_specs=(spec, P(("groups", "member"))),
        check_vma=False,
    )
```

```python
import functools

import jax
import jax.numpy as jnp
from jax import lax
from jax.experimental import pallas as pl
from jax.experimental.pallas import tpu as pltpu
from jax.sharding import PartitionSpec as P

TIME_STEP = 0.15
DIFFUSION = 0.2
MIXING = 0.1
CORIOLIS = 0.5
BUOYANCY_GAIN = 0.3
STRATIFICATION = 0.3
SATURATION = 0.5
LATENT = 0.5

LANES = 128
PAD = 8
MESH = pl.DeviceIdType.MESH


def advance_block(load, emit, halves, levels, chosen):
    spread = TIME_STEP * DIFFUSION
    mix = TIME_STEP * MIXING
    keep = 1.0 - TIME_STEP * (4.0 * DIFFUSION + 2.0 * MIXING)
    lane = lax.broadcasted_iota(jnp.int32, (8, LANES), 1)

    def shifted(parts, k):
        turned = [pltpu.roll(part, k % LANES, 1) for part in parts]
        wrapped = (lane >= LANES + k) if k < 0 else (lane < k)
        step = 1 if k < 0 else -1
        return [jnp.where(wrapped, turned[(h + step) % halves], turned[h]) for h in range(halves)]

    for level in range(levels):
        centre = [[load(field, level, h, 0) for h in range(halves)] for field in range(4)]
        weights = []
        for h in range(halves):
            east, north = centre[0][h], centre[1][h]
            east_eight = east * (TIME_STEP * 8.0 / 12.0)
            north_eight = north * (TIME_STEP * 8.0 / 12.0)
            weights.append((
                east * (TIME_STEP / 12.0), spread - east_eight, spread + east_eight,
                north * (TIME_STEP / 12.0), spread - north_eight, spread + north_eight,
            ))
        updated = {}
        for field in chosen:
            e1, w1, e2, w2 = [shifted(centre[field], k) for k in (-1, 1, -2, 2)]
            news = []
            for h in range(halves):
                east_far, east_near, west_near, north_far, north_near, south_near = weights[h]
                c = centre[field][h]
                n1, s1, n2, s2 = [load(field, level, h, k) for k in (1, -1, 2, -2)]
                edge = (level == 0) + (level == levels - 1)
                beside = [load(field, other, h, 0) for other in (level - 1, level + 1) if 0 <= other < levels]
                new = c * (keep + edge * mix)
                if beside:
                    new = new + functools.reduce(jnp.add, beside) * mix
                new = new + ((e1[h] * east_near + w1[h] * west_near) + (e2[h] - w2[h]) * east_far)
                new = new + ((n1 * north_near + s1 * south_near) + (n2 - s2) * north_far)
                if field == 0:
                    new = new + (TIME_STEP * CORIOLIS) * centre[1][h]
                elif field == 1:
                    new = new + ((TIME_STEP * BUOYANCY_GAIN) * centre[2][h] - (TIME_STEP * CORIOLIS) * centre[0][h])
                elif field == 2:
                    new = new - (TIME_STEP * STRATIFICATION) * centre[1][h]
                news.append(new)
            updated[field] = news
        for h in range(halves):
            if 2 in chosen:
                excess = jnp.maximum(updated[3][h] - SATURATION * jnp.exp(0.1 * updated[2][h]), 0.0)
                updated[2][h] = updated[2][h] + LATENT * excess
                updated[3][h] = updated[3][h] - excess
            for field in chosen:
                emit(field, level, h, updated[field][h])


def kernel(tiles, names, state, pert, out, means,
           ancestors, a, b, early_mid, early_first, early_second, r, p, mine, landed,
           name_sem, load_sem, pert_sem, edge_send, edge_recv, mid_send, mid_recv,
           clone_send, clone_recv, sum_send, sum_recv):
    slots, fields, levels, rows, columns = state.shape
    halves = columns // LANES
    t = lax.axis_index("tile")
    m = lax.axis_index("member")
    has_lo = t > 0
    has_hi = t < tiles - 1
    partner = {"member": 1 - m}
    below = {"tile": t - 1}
    above = {"tile": t + 1}
    early_edges = (early_first, early_second)
    inner = rows - 16
    last = rows - 8

    parts = ((0, 8), (last, 8), (8, inner))

    def load_copy(s, part, h):
        start, size = parts[part]
        return pltpu.make_async_copy(
            state.at[s, :, :, pl.ds(start, size), pl.ds(h * LANES, LANES)],
            a.at[s, :, :, h, pl.ds(PAD + start, size), :], load_sem.at[s, part, h])

    def pert_copy(s, h):
        return pltpu.make_async_copy(
            pert.at[s, :, :, :, pl.ds(h * LANES, LANES)], p.at[s, :, :, h], pert_sem.at[s, h])

    for part in range(3):
        for s in range(slots):
            for h in range(halves):
                load_copy(s, part, h).start()
    for s in range(slots):
        for h in range(halves):
            pert_copy(s, h).start()
    name_copy = pltpu.make_async_copy(names, ancestors, name_sem)
    name_copy.start()

    barrier = pltpu.get_barrier_semaphore()
    pl.semaphore_signal(barrier, inc=1, device_id=partner, device_id_type=MESH)
    for step in range(1, tiles):
        peer = {"tile": lax.rem(t + step, tiles)}
        pl.semaphore_signal(barrier, inc=1, device_id=peer, device_id_type=MESH)

    def remote(src, dst, ssem, rsem, where):
        return pltpu.make_async_remote_copy(
            src_ref=src, dst_ref=dst, send_sem=ssem, recv_sem=rsem, device_id=where, device_id_type=MESH)

    def side_of(turn):
        return lax.rem(t + turn, 2)

    here = (has_lo, has_hi)

    def on_side(turn, act):
        for side in range(2):
            pl.when(jnp.logical_and(side_of(turn) == side, here[side]))(functools.partial(act, side))

    def edge_copies(number, side, s):
        start, at, where = ((0, PAD + rows, below), (rows - 4, PAD - 4, above))[side]
        copies = []
        for h in range(halves):
            if number == 0:
                src, dst = state.at[s, :, :, pl.ds(start, 4), pl.ds(h * LANES, LANES)], a
            else:
                src, dst = r.at[s, :, :, h, pl.ds(PAD + start, 4), :], r
            copies.append(remote(src, dst.at[s, :, :, h, pl.ds(at, 4), :],
                                 edge_send.at[number, s, side, h], edge_recv.at[number, s, side, h], where))
        return copies

    def start_edges(number, turn, s):
        def act(side):
            for copy in edge_copies(number, side, s):
                copy.start()
        on_side(turn, act)

    def wait_edges(number, turn, s):
        def act(side):
            for copy in edge_copies(number, 1 - side, s):
                copy.wait_recv()
        on_side(turn, act)

    def finish_edges(number, turn, s):
        def act(side):
            for copy in edge_copies(number, side, s):
                copy.wait_send()
        on_side(turn, act)

    def clear_edge(ref, turn, s):
        for side, at in ((0, 0), (1, PAD + rows)):
            @pl.when(jnp.logical_and(side_of(turn) == side, jnp.logical_not(here[side])))
            def _():
                ref[s, :, :, :, pl.ds(at, 8), :] = jnp.zeros((fields, levels, halves, 8, LANES), jnp.float32)

    def blocks(count, first, stride, src, s, emit_at, chosen=(0, 1, 2, 3), then=None):
        def one(i, none):
            row = first + i * stride

            def load(field, level, h, shift):
                return src[s, field, level, h, pl.ds(PAD + row + shift, 8), :]

            squares = []

            def emit(field, level, h, value):
                emit_at(i, row, field, level, h, value)
                if field == 2 and then is not None:
                    squares.append(value * value)

            advance_block(load, emit, halves, levels, chosen)
            if squares:
                then(row, functools.reduce(jnp.add, squares))
            return none

        lax.fori_loop(0, count, one, 0)

    def into_b(s):
        def emit_at(i, row, field, level, h, value):
            b[s, field, level, h, pl.ds(PAD + row, 8), :] = value
        return emit_at

    pl.semaphore_wait(barrier, tiles)
    for s in range(slots):
        start_edges(0, 0, s)
    for s in range(slots):
        start_edges(0, 1, s)

    def mid_copy(s):
        own = m * slots + s
        return remote(early_mid.at[own], early_mid.at[own], mid_send.at[s], mid_recv.at[s], partner)

    def early_inner(s, carry):
        for part in range(3):
            for h in range(halves):
                load_copy(s, part, h).wait()
        blocks((rows - 8) // 8, 2, 8, a, s, into_b(s))

        def emit_at(i, row, field, level, h, value):
            early_mid[m * slots + s, field, level, h, pl.ds(pl.multiple_of(i * 8, 8), 8), :] = value

        blocks(inner // 8, 8, 8, b, s, emit_at)
        mid_copy(s).start()
        return carry

    lax.fori_loop(0, slots, early_inner, 0)

    def clone_copy(turn, s):
        own = m * slots + s
        edge = early_edges[turn].at[own]
        return remote(edge, edge, clone_send.at[turn, s], clone_recv.at[turn, s], partner)

    for turn in range(2):
        def early_outer(s, carry):
            wait_edges(0, turn, s)
            clear_edge(a, turn, s)
            blocks(1, side_of(turn) * (rows - 4) - 2, 0, a, s, into_b(s))
            clear_edge(b, turn, s)

            def emit_at(i, row, field, level, h, value):
                early_edges[turn][m * slots + s, field, level, h] = value

            blocks(1, side_of(turn) * last, 0, b, s, emit_at)
            clone_copy(turn, s).start()
            return carry

        lax.fori_loop(0, slots, early_outer, 0)

    name_copy.wait()
    for s in range(slots):
        for h in range(halves):
            pert_copy(s, h).wait()
        mid_copy(s).wait_recv()

    def restart_inner(s, carry):
        source = ancestors[m * slots + s]

        def add(i, none):
            row = pl.multiple_of(i * 8, 8)
            for field in range(fields):
                for level in range(levels):
                    for h in range(halves):
                        r[s, field, level, h, pl.ds(PAD + 8 + row, 8), :] = (
                            early_mid[source, field, level, h, pl.ds(row, 8), :]
                            + p[s, field, level, h, pl.ds(8 + row, 8), :])
            return none

        lax.fori_loop(0, inner // 8, add, 0)
        mine[s] = jnp.zeros((8, LANES), jnp.float32)
        return carry

    for turn in range(2):
        for s in range(slots):
            clone_copy(turn, s).wait_recv()

        def restart_outer(s, carry):
            source = ancestors[m * slots + s]
            at = pl.multiple_of(side_of(turn) * last, 8)
            for field in range(fields):
                for level in range(levels):
                    for h in range(halves):
                        r[s, field, level, h, pl.ds(PAD + at, 8), :] = (
                            early_edges[turn][source, field, level, h] + p[s, field, level, h, pl.ds(at, 8), :])
            start_edges(1, turn, s)
            return carry

        lax.fori_loop(0, slots, restart_outer, 0)
        if turn == 0:
            lax.fori_loop(0, slots, restart_inner, 0)

    def into_out(s):
        def emit_at(i, row, field, level, h, value):
            out[s, field, level, pl.ds(pl.multiple_of(row, 8), 8), pl.ds(h * LANES, LANES)] = value
        return emit_at

    def into_sum(s):
        def then(row, value):
            place = lax.broadcasted_iota(jnp.int32, (8, LANES), 0) + (t * rows + row)
            weight = 1.0 + 2.0 * place.astype(jnp.float32) / (tiles * rows - 1)
            mine[s] = mine[s] + weight * value
        return then

    def late_inner(s, carry):
        blocks((rows - 8) // 8, 2, 8, r, s, into_b(s))
        blocks(inner // 8, 8, 8, b, s, into_out(s), then=into_sum(s))
        return carry

    lax.fori_loop(0, slots, late_inner, 0)

    for turn in range(2):
        def late_outer(s, carry):
            wait_edges(1, turn, s)
            clear_edge(r, turn, s)
            blocks(1, side_of(turn) * (rows - 4) - 2, 0, r, s, into_b(s))
            clear_edge(b, turn, s)
            blocks(1, side_of(turn) * last, 0, b, s, into_out(s), (2, 3), into_sum(s))
            return carry

        lax.fori_loop(0, slots, late_outer, 0)

    sends = [
        remote(mine, landed.at[step - 1], sum_send.at[step - 1], sum_recv.at[step - 1], {"tile": lax.rem(t + step, tiles)})
        for step in range(1, tiles)
    ]
    for copy in sends:
        copy.start()

    def late_winds(s, carry):
        blocks(2, 0, last, b, s, into_out(s), (0, 1))
        return carry

    lax.fori_loop(0, slots, late_winds, 0)
    for s in range(slots):
        for turn in range(2):
            finish_edges(0, turn, s)
            finish_edges(1, turn, s)
            clone_copy(turn, s).wait_send()
        mid_copy(s).wait_send()
    for copy in sends:
        copy.wait()
    scale = 1.0 / (levels * tiles * rows * columns)
    for s in range(slots):
        total = mine[s]
        for step in range(tiles - 1):
            total = total + landed[step, s]
        means[s] = jnp.sum(total) * scale


def body(state, pert, ancestors):
    slots, fields, levels, rows, columns = state.shape
    tiles = lax.axis_size("tile")
    halves = columns // LANES
    members = ancestors.shape[0]
    tall = (slots, fields, levels, halves, rows + 2 * PAD, LANES)
    f32 = lambda *shape: pltpu.VMEM(shape, jnp.float32)
    dma = lambda *shape: pltpu.SemaphoreType.DMA(shape)
    outside = pl.BlockSpec(memory_space=pltpu.HBM)
    return pl.pallas_call(
        functools.partial(kernel, tiles),
        out_shape=[
            jax.ShapeDtypeStruct(state.shape, jnp.float32),
            jax.ShapeDtypeStruct((slots,), jnp.float32),
        ],
        in_specs=[outside] * 3,
        out_specs=[pl.BlockSpec(memory_space=pltpu.VMEM), pl.BlockSpec(memory_space=pltpu.SMEM)],
        scratch_shapes=[
            pltpu.SMEM((members,), jnp.int32),
            f32(*tall), f32(*tall),
            f32(members, fields, levels, halves, rows - 16, LANES),
            f32(members, fields, levels, halves, 8, LANES), f32(members, fields, levels, halves, 8, LANES),
            f32(*tall),
            f32(slots, fields, levels, halves, rows, LANES),
            f32(slots, 8, LANES), f32(tiles - 1, slots, 8, LANES),
            pltpu.SemaphoreType.DMA, dma(slots, 3, halves), dma(slots, halves),
            dma(2, slots, 2, halves), dma(2, slots, 2, halves),
            dma(slots), dma(slots), dma(2, slots), dma(2, slots),
            dma(tiles - 1), dma(tiles - 1),
        ],
        compiler_params=pltpu.CompilerParams(
            collective_id=0, has_side_effects=True, vmem_limit_bytes=48 << 20),
        name="event",
    )(*[pltpu.with_memory_space_constraint(x, pltpu.HBM) for x in (ancestors, state, pert)])


def solution(mesh):
    spec = P(("groups", "member"), None, None, "tile", None)
    return jax.shard_map(
        body,
        mesh=mesh,
        in_specs=(spec, spec, P("groups")),
        out_specs=(spec, P(("groups", "member"))),
        check_vma=False,
    )
```

```python
import functools

import jax
import jax.numpy as jnp
from jax import lax
from jax.experimental import pallas as pl
from jax.experimental.pallas import tpu as pltpu
from jax.sharding import PartitionSpec as P

TIME_STEP = 0.15
DIFFUSION = 0.2
MIXING = 0.1
CORIOLIS = 0.5
BUOYANCY_GAIN = 0.3
STRATIFICATION = 0.3
SATURATION = 0.5
LATENT = 0.5

LANES = 128
PAD = 8
MESH = pl.DeviceIdType.MESH


def advance_block(load, emit, halves, levels, chosen):
    spread = TIME_STEP * DIFFUSION
    mix = TIME_STEP * MIXING
    keep = 1.0 - TIME_STEP * (4.0 * DIFFUSION + 2.0 * MIXING)
    lane = lax.broadcasted_iota(jnp.int32, (8, LANES), 1)

    def shifted(parts, k):
        turned = [pltpu.roll(part, k % LANES, 1) for part in parts]
        wrapped = (lane >= LANES + k) if k < 0 else (lane < k)
        step = 1 if k < 0 else -1
        return [jnp.where(wrapped, turned[(h + step) % halves], turned[h]) for h in range(halves)]

    for level in range(levels):
        centre = [[load(field, level, h, 0) for h in range(halves)] for field in range(4)]
        weights = []
        for h in range(halves):
            east, north = centre[0][h], centre[1][h]
            east_eight = east * (TIME_STEP * 8.0 / 12.0)
            north_eight = north * (TIME_STEP * 8.0 / 12.0)
            weights.append((
                east * (TIME_STEP / 12.0), spread - east_eight, spread + east_eight,
                north * (TIME_STEP / 12.0), spread - north_eight, spread + north_eight,
            ))
        updated = {}
        for field in chosen:
            e1, w1, e2, w2 = [shifted(centre[field], k) for k in (-1, 1, -2, 2)]
            news = []
            for h in range(halves):
                east_far, east_near, west_near, north_far, north_near, south_near = weights[h]
                c = centre[field][h]
                n1, s1, n2, s2 = [load(field, level, h, k) for k in (1, -1, 2, -2)]
                edge = (level == 0) + (level == levels - 1)
                beside = [load(field, other, h, 0) for other in (level - 1, level + 1) if 0 <= other < levels]
                new = c * (keep + edge * mix)
                if beside:
                    new = new + functools.reduce(jnp.add, beside) * mix
                new = new + ((e1[h] * east_near + w1[h] * west_near) + (e2[h] - w2[h]) * east_far)
                new = new + ((n1 * north_near + s1 * south_near) + (n2 - s2) * north_far)
                if field == 0:
                    new = new + (TIME_STEP * CORIOLIS) * centre[1][h]
                elif field == 1:
                    new = new + ((TIME_STEP * BUOYANCY_GAIN) * centre[2][h] - (TIME_STEP * CORIOLIS) * centre[0][h])
                elif field == 2:
                    new = new - (TIME_STEP * STRATIFICATION) * centre[1][h]
                news.append(new)
            updated[field] = news
        for h in range(halves):
            if 2 in chosen:
                excess = jnp.maximum(updated[3][h] - SATURATION * jnp.exp(0.1 * updated[2][h]), 0.0)
                updated[2][h] = updated[2][h] + LATENT * excess
                updated[3][h] = updated[3][h] - excess
            for field in chosen:
                emit(field, level, h, updated[field][h])


def kernel(tiles, names, state, pert, out, means,
           ancestors, a, b, early_mid, early_first, early_second, r, p, mine, landed,
           name_sem, load_sem, pert_sem, edge_send, edge_recv, mid_send, mid_recv,
           clone_send, clone_recv, sum_send, sum_recv):
    slots, fields, levels, rows, columns = state.shape
    halves = columns // LANES
    t = lax.axis_index("tile")
    m = lax.axis_index("member")
    has_lo = t > 0
    has_hi = t < tiles - 1
    partner = {"member": 1 - m}
    below = {"tile": t - 1}
    above = {"tile": t + 1}
    early_edges = (early_first, early_second)
    inner = rows - 16
    last = rows - 8

    parts = ((0, 8), (last, 8), (8, inner))

    def load_copy(s, part, h):
        start, size = parts[part]
        return pltpu.make_async_copy(
            state.at[s, :, :, pl.ds(start, size), pl.ds(h * LANES, LANES)],
            a.at[s, :, :, h, pl.ds(PAD + start, size), :], load_sem.at[s, part, h])

    def pert_copy(s, h):
        return pltpu.make_async_copy(
            pert.at[s, :, :, :, pl.ds(h * LANES, LANES)], p.at[s, :, :, h], pert_sem.at[s, h])

    for part in range(3):
        for s in range(slots):
            for h in range(halves):
                load_copy(s, part, h).start()
    for s in range(slots):
        for h in range(halves):
            pert_copy(s, h).start()
    name_copy = pltpu.make_async_copy(names, ancestors, name_sem)
    name_copy.start()

    barrier = pltpu.get_barrier_semaphore()
    pl.semaphore_signal(barrier, inc=1, device_id=partner, device_id_type=MESH)
    for step in range(1, tiles):
        peer = {"tile": lax.rem(t + step, tiles)}
        pl.semaphore_signal(barrier, inc=1, device_id=peer, device_id_type=MESH)

    def remote(src, dst, ssem, rsem, where):
        return pltpu.make_async_remote_copy(
            src_ref=src, dst_ref=dst, send_sem=ssem, recv_sem=rsem, device_id=where, device_id_type=MESH)

    def side_of(turn):
        return lax.rem(t + turn, 2)

    here = (has_lo, has_hi)

    def on_side(turn, act):
        for side in range(2):
            pl.when(jnp.logical_and(side_of(turn) == side, here[side]))(functools.partial(act, side))

    def edge_copies(number, side, s):
        start, at, where = ((0, PAD + rows, below), (rows - 4, PAD - 4, above))[side]
        copies = []
        for h in range(halves):
            if number == 0:
                src, dst = state.at[s, :, :, pl.ds(start, 4), pl.ds(h * LANES, LANES)], a
            else:
                src, dst = r.at[s, :, :, h, pl.ds(PAD + start, 4), :], r
            copies.append(remote(src, dst.at[s, :, :, h, pl.ds(at, 4), :],
                                 edge_send.at[number, s, side, h], edge_recv.at[number, s, side, h], where))
        return copies

    def start_edges(number, turn, s):
        def act(side):
            for copy in edge_copies(number, side, s):
                copy.start()
        on_side(turn, act)

    def wait_edges(number, turn, s):
        def act(side):
            for copy in edge_copies(number, 1 - side, s):
                copy.wait_recv()
        on_side(turn, act)

    def finish_edges(number, turn, s):
        def act(side):
            for copy in edge_copies(number, side, s):
                copy.wait_send()
        on_side(turn, act)

    def clear_edge(ref, turn, s):
        for side, at in ((0, 0), (1, PAD + rows)):
            @pl.when(jnp.logical_and(side_of(turn) == side, jnp.logical_not(here[side])))
            def _():
                ref[s, :, :, :, pl.ds(at, 8), :] = jnp.zeros((fields, levels, halves, 8, LANES), jnp.float32)

    def blocks(count, first, stride, src, s, emit_at, chosen=(0, 1, 2, 3), then=None):
        def one(i, none):
            row = first + i * stride

            def load(field, level, h, shift):
                return src[s, field, level, h, pl.ds(PAD + row + shift, 8), :]

            squares = []

            def emit(field, level, h, value):
                emit_at(i, row, field, level, h, value)
                if field == 2 and then is not None:
                    squares.append(value * value)

            advance_block(load, emit, halves, levels, chosen)
            if squares:
                then(row, functools.reduce(jnp.add, squares))
            return none

        lax.fori_loop(0, count, one, 0)

    def into_b(s):
        def emit_at(i, row, field, level, h, value):
            b[s, field, level, h, pl.ds(PAD + row, 8), :] = value
        return emit_at

    pl.semaphore_wait(barrier, tiles)
    for s in range(slots):
        start_edges(0, 0, s)
    for s in range(slots):
        start_edges(0, 1, s)

    def mid_copy(s):
        own = m * slots + s
        return remote(early_mid.at[own], early_mid.at[own], mid_send.at[s], mid_recv.at[s], partner)

    def early_inner(s, carry):
        for part in range(3):
            for h in range(halves):
                load_copy(s, part, h).wait()
        blocks((rows - 8) // 8, 2, 8, a, s, into_b(s))

        def emit_at(i, row, field, level, h, value):
            early_mid[m * slots + s, field, level, h, pl.ds(pl.multiple_of(i * 8, 8), 8), :] = value

        blocks(inner // 8, 8, 8, b, s, emit_at)
        mid_copy(s).start()
        return carry

    lax.fori_loop(0, slots, early_inner, 0)

    def clone_copy(turn, s):
        own = m * slots + s
        edge = early_edges[turn].at[own]
        return remote(edge, edge, clone_send.at[turn, s], clone_recv.at[turn, s], partner)

    for turn in range(2):
        def early_outer(s, carry):
            wait_edges(0, turn, s)
            clear_edge(a, turn, s)
            blocks(1, side_of(turn) * (rows - 4) - 2, 0, a, s, into_b(s))
            clear_edge(b, turn, s)

            def emit_at(i, row, field, level, h, value):
                early_edges[turn][m * slots + s, field, level, h] = value

            blocks(1, side_of(turn) * last, 0, b, s, emit_at)
            clone_copy(turn, s).start()
            return carry

        lax.fori_loop(0, slots, early_outer, 0)

    name_copy.wait()
    for s in range(slots):
        for h in range(halves):
            pert_copy(s, h).wait()

    def restart_inner(s, carry):
        source = ancestors[m * slots + s]

        def add(i, none):
            row = pl.multiple_of(i * 8, 8)
            for field in range(fields):
                for level in range(levels):
                    for h in range(halves):
                        r[s, field, level, h, pl.ds(PAD + 8 + row, 8), :] = (
                            early_mid[source, field, level, h, pl.ds(row, 8), :]
                            + p[s, field, level, h, pl.ds(8 + row, 8), :])
            return none

        lax.fori_loop(0, inner // 8, add, 0)
        mine[s] = jnp.zeros((8, LANES), jnp.float32)
        return carry

    for turn in range(2):
        for s in range(slots):
            clone_copy(turn, s).wait_recv()

        def restart_outer(s, carry):
            source = ancestors[m * slots + s]
            at = pl.multiple_of(side_of(turn) * last, 8)
            for field in range(fields):
                for level in range(levels):
                    for h in range(halves):
                        r[s, field, level, h, pl.ds(PAD + at, 8), :] = (
                            early_edges[turn][source, field, level, h] + p[s, field, level, h, pl.ds(at, 8), :])
            start_edges(1, turn, s)
            return carry

        lax.fori_loop(0, slots, restart_outer, 0)
        if turn == 0:
            for s in range(slots):
                mid_copy(s).wait_recv()
            lax.fori_loop(0, slots, restart_inner, 0)

    def into_out(s):
        def emit_at(i, row, field, level, h, value):
            out[s, field, level, pl.ds(pl.multiple_of(row, 8), 8), pl.ds(h * LANES, LANES)] = value
        return emit_at

    def into_sum(s):
        def then(row, value):
            place = lax.broadcasted_iota(jnp.int32, (8, LANES), 0) + (t * rows + row)
            weight = 1.0 + 2.0 * place.astype(jnp.float32) / (tiles * rows - 1)
            mine[s] = mine[s] + weight * value
        return then

    def late_inner(s, carry):
        blocks((rows - 8) // 8, 2, 8, r, s, into_b(s))
        blocks(inner // 8, 8, 8, b, s, into_out(s), (2, 3), into_sum(s))
        return carry

    lax.fori_loop(0, slots, late_inner, 0)

    for turn in range(2):
        def late_outer(s, carry):
            wait_edges(1, turn, s)
            clear_edge(r, turn, s)
            blocks(1, side_of(turn) * (rows - 4) - 2, 0, r, s, into_b(s))
            clear_edge(b, turn, s)
            blocks(1, side_of(turn) * last, 0, b, s, into_out(s), (2, 3), into_sum(s))
            return carry

        lax.fori_loop(0, slots, late_outer, 0)

    sends = [
        remote(mine, landed.at[step - 1], sum_send.at[step - 1], sum_recv.at[step - 1], {"tile": lax.rem(t + step, tiles)})
        for step in range(1, tiles)
    ]
    for copy in sends:
        copy.start()

    def late_winds(s, carry):
        blocks(rows // 8, 0, 8, b, s, into_out(s), (0, 1))
        return carry

    lax.fori_loop(0, slots, late_winds, 0)
    for s in range(slots):
        for turn in range(2):
            finish_edges(0, turn, s)
            finish_edges(1, turn, s)
            clone_copy(turn, s).wait_send()
        mid_copy(s).wait_send()
    for copy in sends:
        copy.wait()
    scale = 1.0 / (levels * tiles * rows * columns)
    for s in range(slots):
        total = mine[s]
        for step in range(tiles - 1):
            total = total + landed[step, s]
        means[s] = jnp.sum(total) * scale


def write_kernel(held, sums, evolved, means, sems, sem):
    copies = [
        pltpu.make_async_copy(held.at[s, field], evolved.at[s, field], sems.at[s, field])
        for s in range(held.shape[0]) for field in range(held.shape[1])
    ]
    copies.append(pltpu.make_async_copy(sums, means, sem))
    for copy in copies:
        copy.start()
    for copy in copies:
        copy.wait()


def body(state, pert, ancestors):
    slots, fields, levels, rows, columns = state.shape
    tiles = lax.axis_size("tile")
    halves = columns // LANES
    members = ancestors.shape[0]
    tall = (slots, fields, levels, halves, rows + 2 * PAD, LANES)
    f32 = lambda *shape: pltpu.VMEM(shape, jnp.float32)
    dma = lambda *shape: pltpu.SemaphoreType.DMA(shape)
    outside = pl.BlockSpec(memory_space=pltpu.HBM)
    evolved, means = pl.pallas_call(
        functools.partial(kernel, tiles),
        out_shape=[
            jax.ShapeDtypeStruct(state.shape, jnp.float32),
            jax.ShapeDtypeStruct((slots,), jnp.float32),
        ],
        in_specs=[outside] * 3,
        out_specs=[pl.BlockSpec(memory_space=pltpu.VMEM), pl.BlockSpec(memory_space=pltpu.SMEM)],
        scratch_shapes=[
            pltpu.SMEM((members,), jnp.int32),
            f32(*tall), f32(*tall),
            f32(members, fields, levels, halves, rows - 16, LANES),
            f32(members, fields, levels, halves, 8, LANES), f32(members, fields, levels, halves, 8, LANES),
            f32(*tall),
            f32(slots, fields, levels, halves, rows, LANES),
            f32(slots, 8, LANES), f32(tiles - 1, slots, 8, LANES),
            pltpu.SemaphoreType.DMA, dma(slots, 3, halves), dma(slots, halves),
            dma(2, slots, 2, halves), dma(2, slots, 2, halves),
            dma(slots), dma(slots), dma(2, slots), dma(2, slots),
            dma(tiles - 1), dma(tiles - 1),
        ],
        compiler_params=pltpu.CompilerParams(
            collective_id=0, has_side_effects=True, vmem_limit_bytes=48 << 20),
        name="event",
    )(*[pltpu.with_memory_space_constraint(x, pltpu.HBM) for x in (ancestors, state, pert)])
    return pl.pallas_call(
        write_kernel,
        out_shape=[
            jax.ShapeDtypeStruct(state.shape, jnp.float32),
            jax.ShapeDtypeStruct((slots,), jnp.float32),
        ],
        in_specs=[pl.BlockSpec(memory_space=pl.ANY), pl.BlockSpec(memory_space=pl.ANY)],
        out_specs=[pl.BlockSpec(memory_space=pl.ANY), pl.BlockSpec(memory_space=pl.ANY)],
        scratch_shapes=[dma(slots, fields), pltpu.SemaphoreType.DMA],
        compiler_params=pltpu.CompilerParams(vmem_limit_bytes=1 << 20),
        name="write",
    )(evolved, means)


def solution(mesh):
    spec = P(("groups", "member"), None, None, "tile", None)
    return jax.shard_map(
        body,
        mesh=mesh,
        in_specs=(spec, spec, P("groups")),
        out_specs=(spec, P(("groups", "member"))),
        check_vma=False,
    )
```

```python
import functools

import jax
import jax.numpy as jnp
from jax import lax
from jax.experimental import pallas as pl
from jax.experimental.pallas import tpu as pltpu
from jax.sharding import PartitionSpec as P

TIME_STEP = 0.15
DIFFUSION = 0.2
MIXING = 0.1
CORIOLIS = 0.5
BUOYANCY_GAIN = 0.3
STRATIFICATION = 0.3
SATURATION = 0.5
LATENT = 0.5

LANES = 128
PAD = 8
MESH = pl.DeviceIdType.MESH


def advance_block(load, emit, halves, levels, chosen):
    spread = TIME_STEP * DIFFUSION
    mix = TIME_STEP * MIXING
    keep = 1.0 - TIME_STEP * (4.0 * DIFFUSION + 2.0 * MIXING)
    lane = lax.broadcasted_iota(jnp.int32, (8, LANES), 1)

    def shifted(parts, k):
        turned = [pltpu.roll(part, k % LANES, 1) for part in parts]
        wrapped = (lane >= LANES + k) if k < 0 else (lane < k)
        step = 1 if k < 0 else -1
        return [jnp.where(wrapped, turned[(h + step) % halves], turned[h]) for h in range(halves)]

    for level in range(levels):
        centre = [[load(field, level, h, 0) for h in range(halves)] for field in range(4)]
        weights = []
        for h in range(halves):
            east, north = centre[0][h], centre[1][h]
            east_eight = east * (TIME_STEP * 8.0 / 12.0)
            north_eight = north * (TIME_STEP * 8.0 / 12.0)
            weights.append((
                east * (TIME_STEP / 12.0), spread - east_eight, spread + east_eight,
                north * (TIME_STEP / 12.0), spread - north_eight, spread + north_eight,
            ))
        updated = {}
        for field in chosen:
            e1, w1, e2, w2 = [shifted(centre[field], k) for k in (-1, 1, -2, 2)]
            news = []
            for h in range(halves):
                east_far, east_near, west_near, north_far, north_near, south_near = weights[h]
                c = centre[field][h]
                n1, s1, n2, s2 = [load(field, level, h, k) for k in (1, -1, 2, -2)]
                edge = (level == 0) + (level == levels - 1)
                beside = [load(field, other, h, 0) for other in (level - 1, level + 1) if 0 <= other < levels]
                new = c * (keep + edge * mix)
                if beside:
                    new = new + functools.reduce(jnp.add, beside) * mix
                new = new + ((e1[h] * east_near + w1[h] * west_near) + (e2[h] - w2[h]) * east_far)
                new = new + ((n1 * north_near + s1 * south_near) + (n2 - s2) * north_far)
                if field == 0:
                    new = new + (TIME_STEP * CORIOLIS) * centre[1][h]
                elif field == 1:
                    new = new + ((TIME_STEP * BUOYANCY_GAIN) * centre[2][h] - (TIME_STEP * CORIOLIS) * centre[0][h])
                elif field == 2:
                    new = new - (TIME_STEP * STRATIFICATION) * centre[1][h]
                news.append(new)
            updated[field] = news
        for h in range(halves):
            if 2 in chosen:
                excess = jnp.maximum(updated[3][h] - SATURATION * jnp.exp(0.1 * updated[2][h]), 0.0)
                updated[2][h] = updated[2][h] + LATENT * excess
                updated[3][h] = updated[3][h] - excess
            for field in chosen:
                emit(field, level, h, updated[field][h])


def kernel(tiles, names, state, pert, out, means,
           ancestors, a, b, early_mid, early_first, early_second, r, p, mine, landed,
           entered, name_sem, load_sem, pert_sem, edge_send, edge_recv, mid_send, mid_recv,
           clone_send, clone_recv, sum_send, sum_recv):
    slots, fields, levels, rows, columns = state.shape
    halves = columns // LANES
    t = lax.axis_index("tile")
    m = lax.axis_index("member")
    has_lo = t > 0
    has_hi = t < tiles - 1
    partner = {"member": 1 - m}
    below = {"tile": t - 1}
    above = {"tile": t + 1}
    early_edges = (early_first, early_second)
    inner = rows - 16
    last = rows - 8

    def signal(sem, has, where):
        @pl.when(has)
        def _():
            pl.semaphore_signal(sem, inc=1, device_id=where, device_id_type=MESH)

    def count(reach):
        return (t >= reach).astype(jnp.int32) + (t + reach < tiles).astype(jnp.int32)

    barrier = pltpu.get_barrier_semaphore()
    signal(barrier, has_lo, below)
    signal(barrier, has_hi, above)
    pl.semaphore_signal(barrier, inc=1, device_id=partner, device_id_type=MESH)

    parts = ((0, 8), (last, 8), (8, inner))

    def load_copy(s, part, h):
        start, size = parts[part]
        return pltpu.make_async_copy(
            state.at[s, :, :, pl.ds(start, size), pl.ds(h * LANES, LANES)],
            a.at[s, :, :, h, pl.ds(PAD + start, size), :], load_sem.at[s, part, h])

    def pert_copy(s, h):
        return pltpu.make_async_copy(
            pert.at[s, :, :, :, pl.ds(h * LANES, LANES)], p.at[s, :, :, h], pert_sem.at[s, h])

    for part in range(3):
        for s in range(slots):
            for h in range(halves):
                load_copy(s, part, h).start()
    for s in range(slots):
        for h in range(halves):
            pert_copy(s, h).start()
    name_copy = pltpu.make_async_copy(names, ancestors, name_sem)
    name_copy.start()

    def remote(src, dst, ssem, rsem, where):
        return pltpu.make_async_remote_copy(
            src_ref=src, dst_ref=dst, send_sem=ssem, recv_sem=rsem, device_id=where, device_id_type=MESH)

    def side_of(turn):
        return lax.rem(t + turn, 2)

    here = (has_lo, has_hi)

    def on_side(turn, act):
        for side in range(2):
            pl.when(jnp.logical_and(side_of(turn) == side, here[side]))(functools.partial(act, side))

    def edge_copies(number, side, s):
        start, at, where = ((0, PAD + rows, below), (rows - 4, PAD - 4, above))[side]
        copies = []
        for h in range(halves):
            if number == 0:
                src, dst = state.at[s, :, :, pl.ds(start, 4), pl.ds(h * LANES, LANES)], a
            else:
                src, dst = r.at[s, :, :, h, pl.ds(PAD + start, 4), :], r
            copies.append(remote(src, dst.at[s, :, :, h, pl.ds(at, 4), :],
                                 edge_send.at[number, s, side, h], edge_recv.at[number, s, side, h], where))
        return copies

    def start_edges(number, turn, s):
        def act(side):
            for copy in edge_copies(number, side, s):
                copy.start()
        on_side(turn, act)

    def wait_edges(number, turn, s):
        def act(side):
            for copy in edge_copies(number, 1 - side, s):
                copy.wait_recv()
        on_side(turn, act)

    def finish_edges(number, turn, s):
        def act(side):
            for copy in edge_copies(number, side, s):
                copy.wait_send()
        on_side(turn, act)

    def clear_edge(ref, turn, s):
        for side, at in ((0, 0), (1, PAD + rows)):
            @pl.when(jnp.logical_and(side_of(turn) == side, jnp.logical_not(here[side])))
            def _():
                ref[s, :, :, :, pl.ds(at, 8), :] = jnp.zeros((fields, levels, halves, 8, LANES), jnp.float32)

    def blocks(count, first, stride, src, s, emit_at, chosen=(0, 1, 2, 3), then=None):
        def one(i, none):
            row = first + i * stride

            def load(field, level, h, shift):
                return src[s, field, level, h, pl.ds(PAD + row + shift, 8), :]

            squares = []

            def emit(field, level, h, value):
                emit_at(i, row, field, level, h, value)
                if field == 2 and then is not None:
                    squares.append(value * value)

            advance_block(load, emit, halves, levels, chosen)
            if squares:
                then(row, functools.reduce(jnp.add, squares))
            return none

        lax.fori_loop(0, count, one, 0)

    def into_b(s):
        def emit_at(i, row, field, level, h, value):
            b[s, field, level, h, pl.ds(PAD + row, 8), :] = value
        return emit_at

    pl.semaphore_wait(barrier, 1 + count(1))
    for turn in range(2):
        for s in range(slots):
            start_edges(0, turn, s)

    reaches = [1 << k for k in range((tiles - 1).bit_length())]

    def tell(k):
        signal(entered.at[k], t >= reaches[k], {"tile": t - reaches[k]})
        signal(entered.at[k], t + reaches[k] < tiles, {"tile": t + reaches[k]})

    def hear(k):
        pl.semaphore_wait(entered.at[k], count(reaches[k]))

    tell(0)

    def mid_copy(s):
        own = m * slots + s
        return remote(early_mid.at[own], early_mid.at[own], mid_send.at[s], mid_recv.at[s], partner)

    def early_inner(s, carry):
        for part in range(3):
            for h in range(halves):
                load_copy(s, part, h).wait()
        blocks((rows - 8) // 8, 2, 8, a, s, into_b(s))

        def emit_at(i, row, field, level, h, value):
            early_mid[m * slots + s, field, level, h, pl.ds(pl.multiple_of(i * 8, 8), 8), :] = value

        blocks(inner // 8, 8, 8, b, s, emit_at)
        mid_copy(s).start()
        return carry

    lax.fori_loop(0, slots, early_inner, 0)

    def clone_copy(turn, s):
        own = m * slots + s
        edge = early_edges[turn].at[own]
        return remote(edge, edge, clone_send.at[turn, s], clone_recv.at[turn, s], partner)

    hear(0)
    tell(1)

    for turn in range(2):
        def early_outer(s, carry):
            wait_edges(0, turn, s)
            clear_edge(a, turn, s)
            blocks(1, side_of(turn) * (rows - 4) - 2, 0, a, s, into_b(s))
            clear_edge(b, turn, s)

            def emit_at(i, row, field, level, h, value):
                early_edges[turn][m * slots + s, field, level, h] = value

            blocks(1, side_of(turn) * last, 0, b, s, emit_at)
            clone_copy(turn, s).start()
            return carry

        lax.fori_loop(0, slots, early_outer, 0)

    name_copy.wait()
    for s in range(slots):
        for h in range(halves):
            pert_copy(s, h).wait()

    def restart_inner(s, carry):
        source = ancestors[m * slots + s]

        def add(i, none):
            row = pl.multiple_of(i * 8, 8)
            for field in range(fields):
                for level in range(levels):
                    for h in range(halves):
                        r[s, field, level, h, pl.ds(PAD + 8 + row, 8), :] = (
                            early_mid[source, field, level, h, pl.ds(row, 8), :]
                            + p[s, field, level, h, pl.ds(8 + row, 8), :])
            return none

        lax.fori_loop(0, inner // 8, add, 0)
        mine[s] = jnp.zeros((8, LANES), jnp.float32)
        return carry

    for turn in range(2):
        for s in range(slots):
            clone_copy(turn, s).wait_recv()

        def restart_outer(s, carry):
            source = ancestors[m * slots + s]
            at = pl.multiple_of(side_of(turn) * last, 8)
            for field in range(fields):
                for level in range(levels):
                    for h in range(halves):
                        r[s, field, level, h, pl.ds(PAD + at, 8), :] = (
                            early_edges[turn][source, field, level, h] + p[s, field, level, h, pl.ds(at, 8), :])
            start_edges(1, turn, s)
            return carry

        lax.fori_loop(0, slots, restart_outer, 0)
        if turn == 0:
            for s in range(slots):
                mid_copy(s).wait_recv()
            lax.fori_loop(0, slots, restart_inner, 0)

    def into_out(s):
        def emit_at(i, row, field, level, h, value):
            out[s, field, level, pl.ds(pl.multiple_of(row, 8), 8), pl.ds(h * LANES, LANES)] = value
        return emit_at

    def into_sum(s):
        def then(row, value):
            place = lax.broadcasted_iota(jnp.int32, (8, LANES), 0) + (t * rows + row)
            weight = 1.0 + 2.0 * place.astype(jnp.float32) / (tiles * rows - 1)
            mine[s] = mine[s] + weight * value
        return then

    def late_inner(s, carry):
        blocks((rows - 8) // 8, 2, 8, r, s, into_b(s))
        blocks(inner // 8, 8, 8, b, s, into_out(s), (2, 3), into_sum(s))
        return carry

    for k in range(2, len(reaches)):
        hear(k - 1)
        tell(k)
    lax.fori_loop(0, slots, late_inner, 0)
    hear(len(reaches) - 1)

    for turn in range(2):
        def late_outer(s, carry):
            wait_edges(1, turn, s)
            clear_edge(r, turn, s)
            blocks(1, side_of(turn) * (rows - 4) - 2, 0, r, s, into_b(s))
            clear_edge(b, turn, s)
            blocks(1, side_of(turn) * last, 0, b, s, into_out(s), (2, 3), into_sum(s))
            return carry

        lax.fori_loop(0, slots, late_outer, 0)

    sends = [
        remote(mine, landed.at[step - 1], sum_send.at[step - 1], sum_recv.at[step - 1], {"tile": lax.rem(t + step, tiles)})
        for step in range(1, tiles)
    ]
    for copy in sends:
        copy.start()

    def late_winds(s, carry):
        blocks(rows // 8, 0, 8, b, s, into_out(s), (0, 1))
        return carry

    lax.fori_loop(0, slots, late_winds, 0)
    for s in range(slots):
        for turn in range(2):
            finish_edges(0, turn, s)
            finish_edges(1, turn, s)
            clone_copy(turn, s).wait_send()
        mid_copy(s).wait_send()
    for copy in sends:
        copy.wait()
    scale = 1.0 / (levels * tiles * rows * columns)
    for s in range(slots):
        total = mine[s]
        for step in range(tiles - 1):
            total = total + landed[step, s]
        means[s] = jnp.sum(total) * scale


def write_kernel(held, sums, evolved, means, sems, sem):
    copies = [
        pltpu.make_async_copy(held.at[s, field], evolved.at[s, field], sems.at[s, field])
        for s in range(held.shape[0]) for field in range(held.shape[1])
    ]
    copies.append(pltpu.make_async_copy(sums, means, sem))
    for copy in copies:
        copy.start()
    for copy in copies:
        copy.wait()


def body(state, pert, ancestors):
    slots, fields, levels, rows, columns = state.shape
    tiles = lax.axis_size("tile")
    halves = columns // LANES
    members = ancestors.shape[0]
    tall = (slots, fields, levels, halves, rows + 2 * PAD, LANES)
    f32 = lambda *shape: pltpu.VMEM(shape, jnp.float32)
    dma = lambda *shape: pltpu.SemaphoreType.DMA(shape)
    outside = pl.BlockSpec(memory_space=pltpu.HBM)
    evolved, means = pl.pallas_call(
        functools.partial(kernel, tiles),
        out_shape=[
            jax.ShapeDtypeStruct(state.shape, jnp.float32),
            jax.ShapeDtypeStruct((slots,), jnp.float32),
        ],
        in_specs=[outside] * 3,
        out_specs=[pl.BlockSpec(memory_space=pltpu.VMEM), pl.BlockSpec(memory_space=pltpu.SMEM)],
        scratch_shapes=[
            pltpu.SMEM((members,), jnp.int32),
            f32(*tall), f32(*tall),
            f32(members, fields, levels, halves, rows - 16, LANES),
            f32(members, fields, levels, halves, 8, LANES), f32(members, fields, levels, halves, 8, LANES),
            f32(*tall),
            f32(slots, fields, levels, halves, rows, LANES),
            f32(slots, 8, LANES), f32(tiles - 1, slots, 8, LANES),
            pltpu.SemaphoreType.REGULAR(((tiles - 1).bit_length(),)), pltpu.SemaphoreType.DMA, dma(slots, 3, halves), dma(slots, halves),
            dma(2, slots, 2, halves), dma(2, slots, 2, halves),
            dma(slots), dma(slots), dma(2, slots), dma(2, slots),
            dma(tiles - 1), dma(tiles - 1),
        ],
        compiler_params=pltpu.CompilerParams(
            collective_id=0, has_side_effects=True, vmem_limit_bytes=48 << 20),
        name="event",
    )(*[pltpu.with_memory_space_constraint(x, pltpu.HBM) for x in (ancestors, state, pert)])
    return pl.pallas_call(
        write_kernel,
        out_shape=[
            jax.ShapeDtypeStruct(state.shape, jnp.float32),
            jax.ShapeDtypeStruct((slots,), jnp.float32),
        ],
        in_specs=[pl.BlockSpec(memory_space=pl.ANY), pl.BlockSpec(memory_space=pl.ANY)],
        out_specs=[pl.BlockSpec(memory_space=pl.ANY), pl.BlockSpec(memory_space=pl.ANY)],
        scratch_shapes=[dma(slots, fields), pltpu.SemaphoreType.DMA],
        compiler_params=pltpu.CompilerParams(vmem_limit_bytes=1 << 20),
        name="write",
    )(evolved, means)


def solution(mesh):
    spec = P(("groups", "member"), None, None, "tile", None)
    return jax.shard_map(
        body,
        mesh=mesh,
        in_specs=(spec, spec, P("groups")),
        out_specs=(spec, P(("groups", "member"))),
        check_vma=False,
    )
```

```python
import functools

import jax
import jax.numpy as jnp
from jax import lax
from jax.experimental import pallas as pl
from jax.experimental.pallas import tpu as pltpu
from jax.sharding import PartitionSpec as P

TIME_STEP = 0.15
DIFFUSION = 0.2
MIXING = 0.1
CORIOLIS = 0.5
BUOYANCY_GAIN = 0.3
STRATIFICATION = 0.3
SATURATION = 0.5
LATENT = 0.5

LANES = 128
PAD = 8
MESH = pl.DeviceIdType.MESH


def advance_block(load, emit, halves, levels, chosen):
    spread = TIME_STEP * DIFFUSION
    mix = TIME_STEP * MIXING
    keep = 1.0 - TIME_STEP * (4.0 * DIFFUSION + 2.0 * MIXING)
    lane = lax.broadcasted_iota(jnp.int32, (8, LANES), 1)

    def shifted(parts, k):
        turned = [pltpu.roll(part, k % LANES, 1) for part in parts]
        wrapped = (lane >= LANES + k) if k < 0 else (lane < k)
        step = 1 if k < 0 else -1
        return [jnp.where(wrapped, turned[(h + step) % halves], turned[h]) for h in range(halves)]

    for level in range(levels):
        centre = [[load(field, level, h, 0) for h in range(halves)] for field in range(4)]
        weights = []
        for h in range(halves):
            east, north = centre[0][h], centre[1][h]
            east_eight = east * (TIME_STEP * 8.0 / 12.0)
            north_eight = north * (TIME_STEP * 8.0 / 12.0)
            weights.append((
                east * (TIME_STEP / 12.0), spread - east_eight, spread + east_eight,
                north * (TIME_STEP / 12.0), spread - north_eight, spread + north_eight,
            ))
        updated = {}
        for field in chosen:
            e1, w1, e2, w2 = [shifted(centre[field], k) for k in (-1, 1, -2, 2)]
            news = []
            for h in range(halves):
                east_far, east_near, west_near, north_far, north_near, south_near = weights[h]
                c = centre[field][h]
                n1, s1, n2, s2 = [load(field, level, h, k) for k in (1, -1, 2, -2)]
                edge = (level == 0) + (level == levels - 1)
                beside = [load(field, other, h, 0) for other in (level - 1, level + 1) if 0 <= other < levels]
                new = c * (keep + edge * mix)
                if beside:
                    new = new + functools.reduce(jnp.add, beside) * mix
                new = new + ((e1[h] * east_near + w1[h] * west_near) + (e2[h] - w2[h]) * east_far)
                new = new + ((n1 * north_near + s1 * south_near) + (n2 - s2) * north_far)
                if field == 0:
                    new = new + (TIME_STEP * CORIOLIS) * centre[1][h]
                elif field == 1:
                    new = new + ((TIME_STEP * BUOYANCY_GAIN) * centre[2][h] - (TIME_STEP * CORIOLIS) * centre[0][h])
                elif field == 2:
                    new = new - (TIME_STEP * STRATIFICATION) * centre[1][h]
                news.append(new)
            updated[field] = news
        for h in range(halves):
            if 2 in chosen:
                excess = jnp.maximum(updated[3][h] - SATURATION * jnp.exp(0.1 * updated[2][h]), 0.0)
                updated[2][h] = updated[2][h] + LATENT * excess
                updated[3][h] = updated[3][h] - excess
            for field in chosen:
                emit(field, level, h, updated[field][h])


def kernel(tiles, names, state, pert, out, means,
           ancestors, a, b, early_mid, early_first, early_second, r, p, mine, brief, landed,
           entered, name_sem, load_sem, pert_sem, edge_send, edge_recv, mid_send, mid_recv,
           clone_send, clone_recv, sum_send, sum_recv):
    slots, fields, levels, rows, columns = state.shape
    halves = columns // LANES
    t = lax.axis_index("tile")
    m = lax.axis_index("member")
    has_lo = t > 0
    has_hi = t < tiles - 1
    partner = {"member": 1 - m}
    below = {"tile": t - 1}
    above = {"tile": t + 1}
    early_edges = (early_first, early_second)
    inner = rows - 16
    last = rows - 8

    def signal(sem, has, where):
        @pl.when(has)
        def _():
            pl.semaphore_signal(sem, inc=1, device_id=where, device_id_type=MESH)

    def count(reach):
        return (t >= reach).astype(jnp.int32) + (t + reach < tiles).astype(jnp.int32)

    barrier = pltpu.get_barrier_semaphore()
    signal(barrier, has_lo, below)
    signal(barrier, has_hi, above)
    pl.semaphore_signal(barrier, inc=1, device_id=partner, device_id_type=MESH)

    parts = ((0, 8), (last, 8), (8, inner))

    def load_copy(s, part, h):
        start, size = parts[part]
        return pltpu.make_async_copy(
            state.at[s, :, :, pl.ds(start, size), pl.ds(h * LANES, LANES)],
            a.at[s, :, :, h, pl.ds(PAD + start, size), :], load_sem.at[s, part, h])

    def pert_copy(s, h):
        return pltpu.make_async_copy(
            pert.at[s, :, :, :, pl.ds(h * LANES, LANES)], p.at[s, :, :, h], pert_sem.at[s, h])

    for part in range(3):
        for s in range(slots):
            for h in range(halves):
                load_copy(s, part, h).start()
    for s in range(slots):
        for h in range(halves):
            pert_copy(s, h).start()
    name_copy = pltpu.make_async_copy(names, ancestors, name_sem)
    name_copy.start()

    def remote(src, dst, ssem, rsem, where):
        return pltpu.make_async_remote_copy(
            src_ref=src, dst_ref=dst, send_sem=ssem, recv_sem=rsem, device_id=where, device_id_type=MESH)

    def side_of(turn):
        return lax.rem(t + turn, 2)

    here = (has_lo, has_hi)

    def on_side(turn, act):
        for side in range(2):
            pl.when(jnp.logical_and(side_of(turn) == side, here[side]))(functools.partial(act, side))

    def edge_copies(number, side, s):
        start, at, where = ((0, PAD + rows, below), (rows - 4, PAD - 4, above))[side]
        held = (a, r)[number]
        return [remote(held.at[s, :, :, :, pl.ds(PAD + start, 4), :], held.at[s, :, :, :, pl.ds(at, 4), :],
                       edge_send.at[number, s, side], edge_recv.at[number, s, side], where)]

    def start_edges(number, turn, s):
        def act(side):
            for copy in edge_copies(number, side, s):
                copy.start()
        on_side(turn, act)

    def wait_edges(number, turn, s):
        def act(side):
            for copy in edge_copies(number, 1 - side, s):
                copy.wait_recv()
        on_side(turn, act)

    def finish_edges(number, turn, s):
        def act(side):
            for copy in edge_copies(number, side, s):
                copy.wait_send()
        on_side(turn, act)

    def clear_edge(ref, turn, s):
        for side, at in ((0, 0), (1, PAD + rows)):
            @pl.when(jnp.logical_and(side_of(turn) == side, jnp.logical_not(here[side])))
            def _():
                ref[s, :, :, :, pl.ds(at, 8), :] = jnp.zeros((fields, levels, halves, 8, LANES), jnp.float32)

    def blocks(count, first, stride, src, s, emit_at, chosen=(0, 1, 2, 3), then=None):
        def one(i, none):
            row = first + i * stride

            def load(field, level, h, shift):
                return src[s, field, level, h, pl.ds(PAD + row + shift, 8), :]

            squares = []

            def emit(field, level, h, value):
                emit_at(i, row, field, level, h, value)
                if field == 2 and then is not None:
                    squares.append(value * value)

            advance_block(load, emit, halves, levels, chosen)
            if squares:
                then(row, functools.reduce(jnp.add, squares))
            return none

        lax.fori_loop(0, count, one, 0)

    def into_b(s):
        def emit_at(i, row, field, level, h, value):
            b[s, field, level, h, pl.ds(PAD + row, 8), :] = value
        return emit_at

    for part in range(2):
        for s in range(slots):
            for h in range(halves):
                load_copy(s, part, h).wait()
    pl.semaphore_wait(barrier, 1 + count(1))
    for turn in range(2):
        for s in range(slots):
            start_edges(0, turn, s)

    reaches = [1 << k for k in range((tiles - 1).bit_length())]

    def tell(k):
        signal(entered.at[k], t >= reaches[k], {"tile": t - reaches[k]})
        signal(entered.at[k], t + reaches[k] < tiles, {"tile": t + reaches[k]})

    def hear(k):
        pl.semaphore_wait(entered.at[k], count(reaches[k]))

    tell(0)

    def mid_copy(s):
        own = m * slots + s
        return remote(early_mid.at[own], early_mid.at[own], mid_send.at[s], mid_recv.at[s], partner)

    def early_inner(s, carry):
        for h in range(halves):
            load_copy(s, 2, h).wait()
        blocks((rows - 8) // 8, 2, 8, a, s, into_b(s))

        def emit_at(i, row, field, level, h, value):
            early_mid[m * slots + s, field, level, h, pl.ds(pl.multiple_of(i * 8, 8), 8), :] = value

        blocks(inner // 8, 8, 8, b, s, emit_at)
        mid_copy(s).start()
        return carry

    lax.fori_loop(0, slots, early_inner, 0)

    def clone_copy(turn, s):
        own = m * slots + s
        edge = early_edges[turn].at[own]
        return remote(edge, edge, clone_send.at[turn, s], clone_recv.at[turn, s], partner)

    hear(0)
    tell(1)

    def early_outer_side(turn, s):
        wait_edges(0, turn, s)
        clear_edge(a, turn, s)
        blocks(1, side_of(turn) * (rows - 4) - 2, 0, a, s, into_b(s))
        clear_edge(b, turn, s)

        def emit_at(i, row, field, level, h, value):
            early_edges[turn][m * slots + s, field, level, h] = value

        blocks(1, side_of(turn) * last, 0, b, s, emit_at)
        clone_copy(turn, s).start()

    def early_outer(s, carry):
        for turn in range(2):
            early_outer_side(turn, s)
        return carry

    lax.fori_loop(0, slots, early_outer, 0)

    name_copy.wait()
    for s in range(slots):
        for h in range(halves):
            pert_copy(s, h).wait()

    def restart_inner(s, carry):
        source = ancestors[m * slots + s]

        def add(i, none):
            row = pl.multiple_of(i * 8, 8)
            for field in range(fields):
                for level in range(levels):
                    for h in range(halves):
                        r[s, field, level, h, pl.ds(PAD + 8 + row, 8), :] = (
                            early_mid[source, field, level, h, pl.ds(row, 8), :]
                            + p[s, field, level, h, pl.ds(8 + row, 8), :])
            return none

        lax.fori_loop(0, inner // 8, add, 0)
        mine[s] = jnp.zeros((8, LANES), jnp.float32)
        return carry

    for turn in range(2):
        for s in range(slots):
            clone_copy(turn, s).wait_recv()

        def restart_outer(s, carry):
            source = ancestors[m * slots + s]
            at = pl.multiple_of(side_of(turn) * last, 8)
            for field in range(fields):
                for level in range(levels):
                    for h in range(halves):
                        r[s, field, level, h, pl.ds(PAD + at, 8), :] = (
                            early_edges[turn][source, field, level, h] + p[s, field, level, h, pl.ds(at, 8), :])
            start_edges(1, turn, s)
            return carry

        lax.fori_loop(0, slots, restart_outer, 0)
        if turn == 0:
            for s in range(slots):
                mid_copy(s).wait_recv()
            lax.fori_loop(0, slots, restart_inner, 0)

    def into_out(s):
        def emit_at(i, row, field, level, h, value):
            out[s, field, level, pl.ds(pl.multiple_of(row, 8), 8), pl.ds(h * LANES, LANES)] = value
        return emit_at

    def into_sum(s):
        def then(row, value):
            place = lax.broadcasted_iota(jnp.int32, (8, LANES), 0) + (t * rows + row)
            weight = 1.0 + 2.0 * place.astype(jnp.float32) / (tiles * rows - 1)
            mine[s] = mine[s] + weight * value
        return then

    def late_inner(s, carry):
        blocks((rows - 8) // 8, 2, 8, r, s, into_b(s))
        blocks(inner // 8, 8, 8, b, s, into_out(s), (2, 3), into_sum(s))
        return carry

    for k in range(2, len(reaches)):
        hear(k - 1)
        tell(k)
    lax.fori_loop(0, slots, late_inner, 0)
    hear(len(reaches) - 1)

    def late_outer_side(turn, s):
        wait_edges(1, turn, s)
        clear_edge(r, turn, s)
        blocks(1, side_of(turn) * (rows - 4) - 2, 0, r, s, into_b(s))
        clear_edge(b, turn, s)
        blocks(1, side_of(turn) * last, 0, b, s, into_out(s), (2, 3), into_sum(s))

    def late_outer(s, carry):
        for turn in range(2):
            late_outer_side(turn, s)
        return carry

    lax.fori_loop(0, slots, late_outer, 0)

    for s in range(slots):
        brief[pl.ds(s, 1), :] = jnp.sum(mine[s], axis=0, keepdims=True)
    sends = [
        remote(brief.at[pl.ds(0, slots)], landed.at[step - 1, pl.ds(0, slots)], sum_send.at[step - 1], sum_recv.at[step - 1], {"tile": lax.rem(t + step, tiles)})
        for step in range(1, tiles)
    ]
    for copy in sends:
        copy.start()

    def late_winds(s, carry):
        blocks(rows // 8, 0, 8, b, s, into_out(s), (0, 1))
        return carry

    lax.fori_loop(0, slots, late_winds, 0)
    for s in range(slots):
        for turn in range(2):
            finish_edges(0, turn, s)
            finish_edges(1, turn, s)
            clone_copy(turn, s).wait_send()
        mid_copy(s).wait_send()
    for copy in sends:
        copy.wait()
    scale = 1.0 / (levels * tiles * rows * columns)
    for s in range(slots):
        total = brief[pl.ds(s, 1), :]
        for step in range(tiles - 1):
            total = total + landed[step, pl.ds(s, 1), :]
        means[s] = jnp.sum(total) * scale


def write_kernel(held, sums, evolved, means, sems, sem):
    copies = [
        pltpu.make_async_copy(held.at[s, field], evolved.at[s, field], sems.at[s, field])
        for s in range(held.shape[0]) for field in range(held.shape[1])
    ]
    copies.append(pltpu.make_async_copy(sums, means, sem))
    for copy in copies:
        copy.start()
    for copy in copies:
        copy.wait()


def body(state, pert, ancestors):
    slots, fields, levels, rows, columns = state.shape
    tiles = lax.axis_size("tile")
    halves = columns // LANES
    members = ancestors.shape[0]
    tall = (slots, fields, levels, halves, rows + 2 * PAD, LANES)
    f32 = lambda *shape: pltpu.VMEM(shape, jnp.float32)
    dma = lambda *shape: pltpu.SemaphoreType.DMA(shape)
    outside = pl.BlockSpec(memory_space=pltpu.HBM)
    evolved, means = pl.pallas_call(
        functools.partial(kernel, tiles),
        out_shape=[
            jax.ShapeDtypeStruct(state.shape, jnp.float32),
            jax.ShapeDtypeStruct((slots,), jnp.float32),
        ],
        in_specs=[outside] * 3,
        out_specs=[pl.BlockSpec(memory_space=pltpu.VMEM), pl.BlockSpec(memory_space=pltpu.SMEM)],
        scratch_shapes=[
            pltpu.SMEM((members,), jnp.int32),
            f32(*tall), f32(*tall),
            f32(members, fields, levels, halves, rows - 16, LANES),
            f32(members, fields, levels, halves, 8, LANES), f32(members, fields, levels, halves, 8, LANES),
            f32(*tall),
            f32(slots, fields, levels, halves, rows, LANES),
            f32(slots, 8, LANES), f32(8, LANES), f32(tiles - 1, 8, LANES),
            pltpu.SemaphoreType.REGULAR(((tiles - 1).bit_length(),)), pltpu.SemaphoreType.DMA, dma(slots, 3, halves), dma(slots, halves),
            dma(2, slots, 2), dma(2, slots, 2),
            dma(slots), dma(slots), dma(2, slots), dma(2, slots),
            dma(tiles - 1), dma(tiles - 1),
        ],
        compiler_params=pltpu.CompilerParams(
            collective_id=0, has_side_effects=True, vmem_limit_bytes=48 << 20),
        name="event",
    )(*[pltpu.with_memory_space_constraint(x, pltpu.HBM) for x in (ancestors, state, pert)])
    return pl.pallas_call(
        write_kernel,
        out_shape=[
            jax.ShapeDtypeStruct(state.shape, jnp.float32),
            jax.ShapeDtypeStruct((slots,), jnp.float32),
        ],
        in_specs=[pl.BlockSpec(memory_space=pl.ANY), pl.BlockSpec(memory_space=pl.ANY)],
        out_specs=[pl.BlockSpec(memory_space=pl.ANY), pl.BlockSpec(memory_space=pl.ANY)],
        scratch_shapes=[dma(slots, fields), pltpu.SemaphoreType.DMA],
        compiler_params=pltpu.CompilerParams(vmem_limit_bytes=1 << 20),
        name="write",
    )(evolved, means)


def solution(mesh):
    spec = P(("groups", "member"), None, None, "tile", None)
    return jax.shard_map(
        body,
        mesh=mesh,
        in_specs=(spec, spec, P("groups")),
        out_specs=(spec, P(("groups", "member"))),
        check_vma=False,
    )
```
